512 devices in a mesh: sky: 32 (over x, z_hi, core), tm: 16 (over z_lo, y).
Axes of the slice: x: 4, y: 4, z: 16 (z_hi: 4, z_lo: 4; z = z_hi * 4 + z_lo), core: 2. Of those that a mesh axis runs over, the one named last changes fastest.
Arguments:
- residuals: float32 [4194304], P(('sky', 'tm')), may hold values from -6 to 6
- weights: float32 [4194304], P(('sky', 'tm')), may hold values from 0.1 to 10
- source_partials: bfloat16 [5, 4194304], P(None, ('sky', 'tm')), may hold values from -1.5 to 1.5
- attitude_partials: bfloat16 [32, 4194304], P(None, ('sky', 'tm')), may hold values from -0.025 to 0.045
- source_index: int32 [4194304], P(('sky', 'tm')), may hold values from 0 to 4095, as said below
- tile_window: int32 [32768], P(('sky', 'tm')), may hold values from 0 to 2047, as said below
- sources: float32 [5, 131072], P(None, 'sky'), may hold values from -6 to 6
- attitude: float32 [2048, 32], P('tm'), may hold values from -6 to 6
- coupling: float32 [2048], P('tm'), may hold values from 1 to 4
Outputs:
- new_sources: float32 [5, 131072], P(None, 'sky')
- new_attitude: float32 [2048, 32], P('tm')
The draws below stay inside these ranges and needn't reach their ends.
Inputs may be any that keep to these rules, and one draw needn't show every extreme that they name: source_index counts among the 4096 sources of the sky region of the device that holds the observation (devices ordered sky first, then tm). The tiles held by the device at tm index t have tile_window from t * 128 to (t + 1) * 128 - 1.
All inputs are finite; a program needn't handle non-finite values.
Results may differ from the reference program's by a relative error of at most 0.00039.
Values sent between devices are 32-bit elements; how exact they have to be, the bound alone decides.
A program may use at most 64 MiB of HBM per device.

```python
import math
import jax
import jax.numpy as jnp
from jax import lax

PARAMS = 5
KNOTS = 32
TILE = 128
ITERS = 8
OBS_DEV = 8192
S_DEV = 4096
W_DEV = 128
SOURCES = 131072
WINDOWS = 2048
OBS = 4194304
TILES_DEV = 64
TILES = 32768
N_TM = 16


def draw_source_index(key, part):
    return jax.random.randint(key, (OBS,), 0, S_DEV, dtype=jnp.int32)


def draw_tile_window(key, part):
    flat = jnp.arange(TILES, dtype=jnp.int32)
    device = flat // TILES_DEV
    time_block = device % N_TM
    offset = jax.random.randint(jax.random.fold_in(key, 7), (TILES,), 0, W_DEV, dtype=jnp.int32)
    return (time_block * W_DEV + offset).astype(jnp.int32)


def draw_attitude_partials(key, part):
    ranking = jax.random.permutation(jax.random.fold_in(key, 11), KNOTS)
    knot_signs = jnp.where(ranking < KNOTS // 2, 1.0, -1.0).astype(jnp.float32)
    common_key = jax.random.fold_in(key, 13)
    jitter_key = jax.random.fold_in(key, 17)
    shared_factor = jnp.clip(jax.random.normal(common_key, (OBS,), jnp.float32), -1.2, 1.2)
    jitter = jax.random.uniform(jitter_key, (KNOTS, OBS), jnp.float32, -0.01, 0.01)
    values = 0.01 + 0.02 * knot_signs[:, None] * shared_factor[None, :] + jitter
    return values.astype(jnp.bfloat16)


def steps_of(key, dims, pieces, least, largest):
    gain = 1.0
    for dim, shards_of in pieces:
        steps = jax.random.uniform(jax.random.fold_in(jax.random.fold_in(key, 6), dim), (shards_of,), jnp.float32, least / len(pieces), largest / len(pieces))
        gain = gain * jnp.repeat(jnp.exp(steps), dims[dim] // shards_of).reshape((-1,) + (1,) * (len(dims) - 1 - dim))
    return gain


def bell_draw(rng, dims, width, most, cuts=(), held_as=jnp.bfloat16):
    array = jax.random.normal(rng, dims, jnp.float32) * width
    if len(cuts) > 0:
        array = steps_of(rng, dims, cuts, -0.22, 0.18) * array
    return jnp.clip(array, min=-most, max=most).astype(held_as)


def setup_inputs(seed: int = 0) -> dict:
    seeds = jax.random.split(jax.random.key(seed), 10)
    residuals = bell_draw(seeds[0], (OBS,), 1.0, 6.0, ((0, 512),), jnp.float32)
    weights = jnp.clip(jnp.exp(math.log(10.0) - 4.6051702 * jax.random.uniform(seeds[1], (OBS,), jnp.float32) ** steps_of(seeds[1], (OBS,), ((0, 512),), -0.2, 0.2)), 0.1, 10.0)
    source_partials = bell_draw(seeds[2], (PARAMS, OBS), 0.25, 1.5, ((1, 512),))
    attitude_partials = draw_attitude_partials(jax.random.fold_in(seeds[9], 71), 0)
    source_index = draw_source_index(jax.random.fold_in(seeds[9], 71), 0)
    tile_window = draw_tile_window(jax.random.fold_in(seeds[9], 71), 0)
    sources = bell_draw(seeds[6], (PARAMS, SOURCES), 1.0, 6.0, ((1, 32),), jnp.float32)
    attitude = bell_draw(seeds[7], (WINDOWS, KNOTS), 1.0, 6.0, ((0, 16),), jnp.float32)
    coupling = jnp.clip(jnp.exp(math.log(4.0) - 1.3862944 * jax.random.uniform(seeds[8], (WINDOWS,), jnp.float32) ** steps_of(seeds[8], (WINDOWS,), ((0, 16),), -0.2, 0.2)), 1.0, 4.0)
    return {"residuals": residuals, "weights": weights, "source_partials": source_partials, "attitude_partials": attitude_partials, "source_index": source_index, "tile_window": tile_window, "sources": sources, "attitude": attitude, "coupling": coupling}


LOWER_PAIRS = tuple(((i, j) for i in range(5) for j in range(i + 1)))
DAMPING = 0.8
HIGHEST = lax.Precision.HIGHEST

def moment_rows(partials, weights, residuals):
    values = partials.astype(jnp.float32)
    entries = [weights * values[i] * values[j] for i, j in LOWER_PAIRS]
    entries = entries + [weights * values[i] * residuals for i in range(5)]
    return jnp.stack(entries)

def solve_sources(moments):
    matrix = {}
    for position, pair in enumerate(LOWER_PAIRS):
        matrix[pair] = moments[position] + (1.0 if pair[0] == pair[1] else 0.0)
    factor = {}
    for i in range(5):
        for j in range(i + 1):
            reduced = matrix[i, j]
            for k in range(j):
                reduced = reduced - factor[i, k] * factor[j, k]
            if i == j:
                factor[i, i] = jnp.sqrt(reduced)
            else:
                factor[i, j] = reduced / factor[j, j]
    forward = []
    for i in range(5):
        current = moments[15 + i]
        for k in range(i):
            current = current - factor[i, k] * forward[k]
        forward.append(current / factor[i, i])
    result = [None] * 5
    for i in reversed(range(5)):
        current = forward[i]
        for k in range(i + 1, 5):
            current = current - factor[k, i] * result[k]
        result[i] = current / factor[i, i]
    return jnp.stack(result)

def window_inverse(symmetric, left_coupling, right_coupling):
    knot_count = symmetric.shape[1]
    identity = jnp.eye(knot_count, dtype=jnp.float32)
    blocks = symmetric + (left_coupling + right_coupling)[:, None, None] * identity
    lower_factor = jnp.linalg.cholesky(blocks)
    inverse_factor = jax.scipy.linalg.solve_triangular(lower_factor, jnp.broadcast_to(identity, blocks.shape), lower=True)
    return jnp.einsum('wlk,wlm->wkm', inverse_factor, inverse_factor, precision=HIGHEST)

def apply_blocks(blocks, vectors):
    return jnp.einsum('wkl,wl->wk', blocks, vectors, precision=HIGHEST)

def global_index(source_index, block):
    start = (block * OBS_DEV).astype(jnp.int32)
    local = lax.dynamic_slice_in_dim(source_index, start, OBS_DEV, 0)
    offset = (block // N_TM * S_DEV).astype(jnp.int32)
    return (local + offset).astype(jnp.int32)

def reference(residuals, weights, source_partials, attitude_partials, source_index, tile_window, sources, attitude, coupling):
    block_total = residuals.shape[0] // OBS_DEV
    tiles_block = OBS_DEV // TILE
    window_total = attitude.shape[0]
    knot_count = attitude.shape[1]

    def source_step(block, moments):
        start = (block * OBS_DEV).astype(jnp.int32)
        part_res = lax.dynamic_slice_in_dim(residuals, start, OBS_DEV, 0)
        part_weight = lax.dynamic_slice_in_dim(weights, start, OBS_DEV, 0)
        part_src = lax.dynamic_slice_in_dim(source_partials, start, OBS_DEV, 1)
        part_index = global_index(source_index, block)
        return moments.at[:, part_index].add(moment_rows(part_src, part_weight, part_res))
    moments = lax.fori_loop(0, block_total, source_step, jnp.zeros((20, sources.shape[1]), jnp.float32))
    source_change = solve_sources(moments)
    new_sources = sources + source_change

    def window_step(block, carry):
        normal, right_side = carry
        start = (block * OBS_DEV).astype(jnp.int32)
        part_res = lax.dynamic_slice_in_dim(residuals, start, OBS_DEV, 0)
        part_weight = lax.dynamic_slice_in_dim(weights, start, OBS_DEV, 0)
        part_src = lax.dynamic_slice_in_dim(source_partials, start, OBS_DEV, 1)
        part_att = lax.dynamic_slice_in_dim(attitude_partials, start, OBS_DEV, 1)
        part_index = global_index(source_index, block)
        picked = source_change[:, part_index]
        corrected = part_res - lax.optimization_barrier(jnp.sum(part_src.astype(jnp.float32) * picked, axis=0))
        weighted = (part_weight * corrected).astype(jnp.bfloat16)
        scaled = (part_weight[None, :] * part_att.astype(jnp.float32)).astype(jnp.bfloat16)
        shaped_att = part_att.reshape(knot_count, tiles_block, TILE).astype(jnp.float32)
        shaped_scaled = scaled.reshape(knot_count, tiles_block, TILE).astype(jnp.float32)
        tile_normal = jnp.einsum('ktp,ltp->tkl', shaped_scaled, shaped_att, precision=HIGHEST).reshape(tiles_block, knot_count * knot_count)
        tile_rhs = jnp.einsum('ktp,tp->tk', shaped_att, weighted.reshape(tiles_block, TILE).astype(jnp.float32), precision=HIGHEST)
        tile_start = (block * tiles_block).astype(jnp.int32)
        windows = lax.dynamic_slice_in_dim(tile_window, tile_start, tiles_block, 0)
        return (normal.at[windows].add(tile_normal), right_side.at[windows].add(tile_rhs))
    start_carry = (jnp.zeros((window_total, knot_count * knot_count), jnp.float32), jnp.zeros((window_total, knot_count), jnp.float32))
    normal, right_side = lax.fori_loop(0, block_total, window_step, start_carry)
    normal = normal.reshape(window_total, knot_count, knot_count)
    symmetric = 0.5 * (normal + jnp.swapaxes(normal, 1, 2))
    zero_one = jnp.zeros((1,), jnp.float32)
    left_coupling = jnp.concatenate([zero_one, coupling[:-1]])
    right_coupling = jnp.concatenate([coupling[:-1], zero_one])
    inverse = window_inverse(symmetric, left_coupling, right_coupling)
    change = DAMPING * apply_blocks(inverse, right_side)
    for sweep in range(ITERS - 1):
        padded = jnp.pad(change, ((1, 1), (0, 0)))
        applied = apply_blocks(symmetric, change) + (left_coupling + right_coupling)[:, None] * change
        applied = applied - left_coupling[:, None] * padded[:-2] - right_coupling[:, None] * padded[2:]
        change = change + DAMPING * apply_blocks(inverse, right_side - applied)
    return (new_sources, attitude + change)
```

```python
import functools

import jax
import jax.numpy as jnp
from jax import lax
from jax.experimental import pallas as pl
from jax.experimental.pallas import tpu as pltpu
from jax.sharding import PartitionSpec as P

TILE = 128
ITERS = 8
BLOCK = 8
LOWER_PAIRS = tuple(((i, j) for i in range(5) for j in range(i + 1)))
DAMPING = 0.8
HIGHEST = lax.Precision.HIGHEST
MESH = pl.DeviceIdType.MESH
VMEM = pl.BlockSpec(memory_space=pltpu.VMEM)


def along_time(count):
    return count, lambda: lax.axis_index("tm"), lambda p: {"tm": p}


def along_plane():
    def spot():
        sky = lax.axis_index("sky")
        return lax.div(sky, 8) * 2 + lax.rem(sky, 2)

    def name(p):
        depth = lax.rem(lax.div(lax.axis_index("sky"), 2), 4)
        return {"sky": lax.div(p, 2) * 8 + depth * 2 + lax.rem(p, 2)}

    return 8, spot, name


def along_depth():
    def spot():
        return lax.rem(lax.div(lax.axis_index("sky"), 2), 4)

    def name(p):
        sky = lax.axis_index("sky")
        return {"sky": lax.div(sky, 8) * 8 + p * 2 + lax.rem(sky, 2)}

    return 4, spot, name


def meet(count, me, name):
    barrier = pltpu.get_barrier_semaphore()
    for step in range(1, count):
        pl.semaphore_signal(
            barrier, inc=1, device_id=name(lax.rem(me + step, count)), device_id_type=MESH
        )
    pl.semaphore_wait(barrier, count - 1)


def sum_kernel(group, finish, x_ref, o_ref, land, send_sem, recv_sem):
    count, spot, name = group
    me = spot()
    meet(count, me, name)
    copies = []
    for step in range(1, count):
        peer = lax.rem(me + step, count)
        copy = pltpu.make_async_remote_copy(
            src_ref=x_ref.at[peer],
            dst_ref=land.at[step - 1],
            send_sem=send_sem.at[step - 1],
            recv_sem=recv_sem.at[step - 1],
            device_id=name(peer),
            device_id_type=MESH,
        )
        copy.start()
        copies.append(copy)
    total = x_ref[me]
    for step in range(1, count):
        copies[step - 1].wait_recv()
        total = total + land[step - 1]
    finish(total, o_ref)
    for copy in copies:
        copy.wait_send()


def spread_kernel(group, x_ref, o_ref, land, send_sem, recv_sem):
    count, spot, name = group
    me = spot()
    meet(count, me, name)
    copies = []
    for step in range(1, count):
        copy = pltpu.make_async_remote_copy(
            src_ref=x_ref,
            dst_ref=land.at[step - 1],
            send_sem=send_sem.at[step - 1],
            recv_sem=recv_sem.at[step - 1],
            device_id=name(lax.rem(me + step, count)),
            device_id_type=MESH,
        )
        copy.start()
        copies.append(copy)
    o_ref[me] = x_ref[...]
    for step in range(1, count):
        copies[step - 1].wait_recv()
        o_ref[lax.rem(me + count - step, count)] = land[step - 1]
    for copy in copies:
        copy.wait_send()


def group_call(kernel, name, count, x, block, out, collective_id):
    return pl.pallas_call(
        kernel,
        name=name,
        out_shape=jax.ShapeDtypeStruct(out, jnp.float32),
        in_specs=[VMEM],
        out_specs=VMEM,
        scratch_shapes=[
            pltpu.VMEM((count - 1,) + block, jnp.float32),
            pltpu.SemaphoreType.DMA((count - 1,)),
            pltpu.SemaphoreType.DMA((count - 1,)),
        ],
        compiler_params=pltpu.CompilerParams(collective_id=collective_id, has_side_effects=True),
    )(x)


def keep(total, o_ref):
    o_ref[...] = total


def summed(x, group, collective_id, finish=keep, rows=None):
    block = x.shape[1:]
    out = block if rows is None else (rows,) + block[1:]
    kernel = functools.partial(sum_kernel, group, finish)
    return group_call(kernel, "summed", group[0], x, block, out, collective_id)


def spread(x, group, collective_id):
    kernel = functools.partial(spread_kernel, group)
    return group_call(kernel, "spread", group[0], x, x.shape, (group[0],) + x.shape, collective_id)


def moment_rows(partials, weights, residuals):
    values = partials.astype(jnp.float32)
    entries = [weights * values[i] * values[j] for i, j in LOWER_PAIRS]
    entries = entries + [weights * values[i] * residuals for i in range(5)]
    return jnp.stack(entries)


def solve_sources(moments):
    matrix = {}
    for position, pair in enumerate(LOWER_PAIRS):
        matrix[pair] = moments[position] + (1.0 if pair[0] == pair[1] else 0.0)
    factor = {}
    for i in range(5):
        for j in range(i + 1):
            reduced = matrix[i, j]
            for k in range(j):
                reduced = reduced - factor[i, k] * factor[j, k]
            if i == j:
                factor[i, i] = jnp.sqrt(reduced)
            else:
                factor[i, j] = reduced / factor[j, j]
    forward = []
    for i in range(5):
        current = moments[15 + i]
        for k in range(i):
            current = current - factor[i, k] * forward[k]
        forward.append(current / factor[i, i])
    result = [None] * 5
    for i in reversed(range(5)):
        current = forward[i]
        for k in range(i + 1, 5):
            current = current - factor[k, i] * result[k]
        result[i] = current / factor[i, i]
    return result


def finish_sources(total, o_ref):
    solved = solve_sources([total[r : r + 1, :] for r in range(20)])
    zero = jnp.zeros_like(solved[0])
    o_ref[...] = jnp.concatenate(solved + [zero] * 3, axis=0)


def applied(inverse, vector, knots):
    parts = [None] * 4
    for row in range(knots):
        term = inverse[row] * vector[row : row + 1, :]
        spot = row % 4
        parts[spot] = term if parts[spot] is None else parts[spot] + term
    return (parts[0] + parts[1]) + (parts[2] + parts[3])


def attitude_kernel(
    knots, count, packed_ref, ties_ref, o_ref, inverse, sent, land, send_sem, recv_sem
):
    me = lax.axis_index("tm")
    after, before = lax.rem(me + 1, count), lax.rem(me + count - 1, count)
    barrier = pltpu.get_barrier_semaphore()
    for peer in (before, after):
        pl.semaphore_signal(barrier, inc=1, device_id={"tm": peer}, device_id_type=MESH)

    left, right = ties_ref[0:1, :], ties_ref[1:2, :]
    lanes = left.shape[1]
    row_ids = lax.broadcasted_iota(jnp.int32, (knots, lanes), 0)
    start = 0
    for group in range(knots // BLOCK):
        width = (group + 1) * BLOCK
        for k in range(group * BLOCK, width):
            row = packed_ref[start : start + width, :]
            row = row + jnp.where(row_ids[:width] == k, left + right, 0.0)
            inverse[k, :width, :] = row
            start += width
    for low in range(knots // BLOCK):
        for high in range(low + 1, knots // BLOCK):
            rows = pl.ds(high * BLOCK, BLOCK)
            for k in range(low * BLOCK, (low + 1) * BLOCK):
                inverse[k, rows, :] = inverse[rows, k, :]
    right_side = packed_ref[start : start + knots, :]

    def pivot(p, carry):
        own = inverse[p]
        here = row_ids == p
        scale = 1.0 / inverse[p, pl.ds(p, 1), :]
        row = jnp.where(here, scale, own * scale)
        for i in range(knots):
            factor = inverse[i, pl.ds(p, 1), :]
            inverse[i] = jnp.where(here, 0.0, inverse[i]) - factor * row
        inverse[p] = row
        return carry

    lax.fori_loop(0, knots, pivot, 0)

    base = DAMPING * applied(inverse, right_side, knots)
    lane_ids = lax.broadcasted_iota(jnp.int32, (knots, lanes), 1)
    change = base
    pl.semaphore_wait(barrier, 2)
    for sweep in range(ITERS - 1):
        sent[sweep] = change
        copies = []
        for side, peer in enumerate((after, before)):
            copy = pltpu.make_async_remote_copy(
                src_ref=sent.at[sweep],
                dst_ref=land.at[sweep, side],
                send_sem=send_sem.at[sweep, side],
                recv_sem=recv_sem.at[sweep, side],
                device_id={"tm": peer},
                device_id_type=MESH,
            )
            copy.start()
            copies.append(copy)
        own_low, own_high = pltpu.roll(change, 1, 1), pltpu.roll(change, lanes - 1, 1)
        for copy in copies:
            copy.wait()
        low = jnp.where(lane_ids == 0, pltpu.roll(land[sweep, 0], 1, 1), own_low)
        high = jnp.where(
            lane_ids == lanes - 1, pltpu.roll(land[sweep, 1], lanes - 1, 1), own_high
        )
        tied = left * low + right * high
        change = (1.0 - DAMPING) * change + base + DAMPING * applied(inverse, tied, knots)
    o_ref[...] = change


def attitude_change(packed, ties, knots, count):
    lanes = ties.shape[1]
    sweeps = ITERS - 1
    return pl.pallas_call(
        functools.partial(attitude_kernel, knots, count),
        name="attitude_change",
        out_shape=jax.ShapeDtypeStruct((knots, lanes), jnp.float32),
        in_specs=[VMEM, VMEM],
        out_specs=VMEM,
        scratch_shapes=[
            pltpu.VMEM((knots, knots, lanes), jnp.float32),
            pltpu.VMEM((sweeps, knots, lanes), jnp.float32),
            pltpu.VMEM((sweeps, 2, knots, lanes), jnp.float32),
            pltpu.SemaphoreType.DMA((sweeps, 2)),
            pltpu.SemaphoreType.DMA((sweeps, 2)),
        ],
        compiler_params=pltpu.CompilerParams(collective_id=7, has_side_effects=True),
    )(packed, ties)


def on_device(
    residuals,
    weights,
    source_partials,
    attitude_partials,
    source_index,
    tile_window,
    sources,
    attitude,
    coupling,
):
    source_count = sources.shape[1]
    window_count, knot_count = attitude.shape
    tile_count = attitude_partials.shape[1] // TILE
    times = lax.axis_size("tm")
    time_group = along_time(times)

    summands = moment_rows(source_partials, weights, residuals)
    moments = jnp.zeros((20, source_count), jnp.float32).at[:, source_index].add(summands)
    moments = moments.reshape(20, times, source_count // times).transpose(1, 0, 2)
    owned = summed(moments, time_group, 1, finish_sources, 8)
    source_change = spread(owned, time_group, 2)
    source_change = source_change[:, :5].transpose(1, 0, 2).reshape(5, source_count)
    new_sources = sources + source_change

    scaled = (weights[None, :] * attitude_partials.astype(jnp.float32)).astype(jnp.bfloat16)
    shaped_att = attitude_partials.reshape(knot_count, tile_count, TILE)
    tile_normal = jnp.einsum(
        "ktp,ltp->tkl",
        scaled.reshape(knot_count, tile_count, TILE),
        shaped_att,
        preferred_element_type=jnp.float32,
    )
    tile_normal = 0.5 * (tile_normal + jnp.swapaxes(tile_normal, 1, 2))
    tile_lower = jnp.concatenate(
        [
            tile_normal[:, b : b + BLOCK, : b + BLOCK].reshape(tile_count, -1)
            for b in range(0, knot_count, BLOCK)
        ],
        axis=1,
    )

    picked = source_change[:, source_index]
    corrected = residuals - jnp.sum(source_partials.astype(jnp.float32) * picked, axis=0)
    weighted = (weights * corrected).astype(jnp.bfloat16)
    tile_rhs = jnp.einsum(
        "ktp,tp->tk",
        shaped_att,
        weighted.reshape(tile_count, TILE),
        preferred_element_type=jnp.float32,
    )
    tile_rows = jnp.concatenate([tile_lower, tile_rhs], axis=1)
    first_window = lax.axis_index("tm") * window_count
    window_ids = lax.broadcasted_iota(jnp.int32, (tile_count, window_count), 1)
    selector = (tile_window[:, None] - first_window == window_ids).astype(jnp.float32)
    packed = lax.dot_general(
        tile_rows, selector, (((0,), (0,)), ((), ())), precision=HIGHEST
    )
    packed = jnp.pad(packed, ((0, 768 - packed.shape[0]), (0, 0)))

    plane, depth = along_plane(), along_depth()
    part = summed(packed.reshape(8, 96, window_count), plane, 3)
    part = summed(part.reshape(4, 24, window_count), depth, 4)
    part = spread(part, depth, 5).reshape(96, window_count)
    packed = spread(part, plane, 6).reshape(768, window_count)

    earlier = lax.ppermute(coupling[-1:], "tm", [(i, i + 1) for i in range(times - 1)])
    left = jnp.concatenate([earlier, coupling[:-1]])
    is_final = lax.axis_index("tm") == times - 1
    final_slot = lax.broadcasted_iota(jnp.int32, (window_count,), 0) == window_count - 1
    right = jnp.where(jnp.logical_and(is_final, final_slot), 0.0, coupling)
    change = attitude_change(packed, jnp.stack([left, right]), knot_count, times)
    return (new_sources, attitude + change.T)


def solution(mesh):
    return jax.shard_map(
        on_device,
        mesh=mesh,
        in_specs=(
            P(("sky", "tm")),
            P(("sky", "tm")),
            P(None, ("sky", "tm")),
            P(None, ("sky", "tm")),
            P(("sky", "tm")),
            P(("sky", "tm")),
            P(None, "sky"),
            P("tm", None),
            P("tm"),
        ),
        out_specs=(P(None, "sky"), P("tm", None)),
        check_vma=False,
    )
```

```python
import functools

import jax
import jax.numpy as jnp
from jax import lax
from jax.experimental import pallas as pl
from jax.experimental.pallas import tpu as pltpu
from jax.sharding import PartitionSpec as P

TILE = 128
ITERS = 8
BLOCK = 8
PIECE = 24
LOWER_PAIRS = tuple(((i, j) for i in range(5) for j in range(i + 1)))
DAMPING = 0.8
HIGHEST = lax.Precision.HIGHEST
MESH = pl.DeviceIdType.MESH
VMEM = pl.BlockSpec(memory_space=pltpu.VMEM)


def along_time(count):
    return count, lambda: lax.axis_index("tm"), lambda p: {"tm": p}


def along_plane():
    def spot():
        sky = lax.axis_index("sky")
        return lax.div(sky, 8) * 2 + lax.rem(sky, 2)

    def name(p):
        depth = lax.rem(lax.div(lax.axis_index("sky"), 2), 4)
        return {"sky": lax.div(p, 2) * 8 + depth * 2 + lax.rem(p, 2)}

    return 8, spot, name


def along_depth():
    def spot():
        return lax.rem(lax.div(lax.axis_index("sky"), 2), 4)

    def name(p):
        sky = lax.axis_index("sky")
        return {"sky": lax.div(sky, 8) * 8 + p * 2 + lax.rem(sky, 2)}

    return 4, spot, name


def signal_all(barrier, group):
    count, spot, name = group
    me = spot()
    for step in range(1, count):
        peer = lax.rem(me + step, count)
        pl.semaphore_signal(barrier, inc=1, device_id=name(peer), device_id_type=MESH)
    return count - 1


def send_all(group, source, land, send_sem, recv_sem):
    count, spot, name = group
    me = spot()
    copies = []
    for step in range(1, count):
        peer = lax.rem(me + step, count)
        copy = pltpu.make_async_remote_copy(
            src_ref=source(peer),
            dst_ref=land.at[step - 1],
            send_sem=send_sem.at[step - 1],
            recv_sem=recv_sem.at[step - 1],
            device_id=name(peer),
            device_id_type=MESH,
        )
        copy.start()
        copies.append(copy)
    return copies


def sum_stage(group, x_ref, land, send_sem, recv_sem):
    copies = send_all(group, lambda peer: x_ref.at[peer], land, send_sem, recv_sem)
    total = x_ref[group[1]()]
    for step, copy in enumerate(copies):
        copy.wait_recv()
        total = total + land[step]
    for copy in copies:
        copy.wait_send()
    return total


def spread_stage(group, x_ref, land, send_sem, recv_sem, place):
    count, spot, _ = group
    me = spot()
    copies = send_all(group, lambda peer: x_ref, land, send_sem, recv_sem)
    place(me, x_ref[...])
    for step, copy in enumerate(copies):
        copy.wait_recv()
        place(lax.rem(me + count - step - 1, count), land[step])
    for copy in copies:
        copy.wait_send()


def stage_scratch(group, block):
    peers = group[0] - 1
    return [
        pltpu.VMEM((peers,) + block, jnp.float32),
        pltpu.SemaphoreType.DMA((peers,)),
        pltpu.SemaphoreType.DMA((peers,)),
    ]


def solve_sources(moments):
    matrix = {}
    for position, pair in enumerate(LOWER_PAIRS):
        matrix[pair] = moments[position] + (1.0 if pair[0] == pair[1] else 0.0)
    factor = {}
    for i in range(5):
        for j in range(i + 1):
            reduced = matrix[i, j]
            for k in range(j):
                reduced = reduced - factor[i, k] * factor[j, k]
            if i == j:
                factor[i, i] = jnp.sqrt(reduced)
            else:
                factor[i, j] = reduced / factor[j, j]
    forward = []
    for i in range(5):
        current = moments[15 + i]
        for k in range(i):
            current = current - factor[i, k] * forward[k]
        forward.append(current / factor[i, i])
    result = [None] * 5
    for i in reversed(range(5)):
        current = forward[i]
        for k in range(i + 1, 5):
            current = current - factor[k, i] * result[k]
        result[i] = current / factor[i, i]
    return result


CHUNK = 1024
LOW = 256
ROWS = 24


def two_parts(values):
    high = values.astype(jnp.bfloat16)
    return high, (values - high.astype(jnp.float32)).astype(jnp.bfloat16)


def chosen(index, count):
    ids = lax.broadcasted_iota(jnp.int32, (count, index.shape[1]), 0)
    return (ids == index).astype(jnp.float32)


def source_kernel(
    group,
    residuals_ref,
    weights_ref,
    partials_ref,
    index_ref,
    sources_ref,
    new_ref,
    weighted_ref,
    total_ref,
    moments,
    solved_ref,
    changes,
    land_sum,
    send_sum,
    recv_sum,
    land_spread,
    send_spread,
    recv_spread,
):
    count = group[0]
    barrier = pltpu.get_barrier_semaphore()
    peers = signal_all(barrier, group)
    chunks = residuals_ref.shape[1] // CHUNK
    total_ref[...] = jnp.zeros_like(total_ref)

    def gather_sums(chunk, carry):
        span = pl.ds(pl.multiple_of(chunk * CHUNK, CHUNK), CHUNK)
        index = index_ref[:, span]
        weights = weights_ref[:, span]
        residuals = residuals_ref[:, span]
        values = partials_ref[:, span].astype(jnp.float32)
        rows = [values[i : i + 1, :] for i in range(5)]
        scaled = [weights * row for row in rows]
        entries = [scaled[i] * rows[j] for i, j in LOWER_PAIRS]
        entries = entries + [scaled[i] * residuals for i in range(5)]
        entries = entries + [jnp.zeros_like(weights)] * (ROWS - 20)
        high, low = two_parts(jnp.concatenate(entries, axis=0))
        both = jnp.concatenate([high, low], axis=0)
        owner = chosen(lax.div(index, LOW), count)
        held = [both * owner[h : h + 1, :].astype(jnp.bfloat16) for h in range(count)]
        held = jnp.concatenate(held, axis=0)
        picks = chosen(lax.rem(index, LOW), LOW).astype(jnp.bfloat16)
        total_ref[...] += lax.dot_general(
            held, picks, (((1,), (1,)), ((), ())), preferred_element_type=jnp.float32
        )
        return carry

    lax.fori_loop(0, chunks, gather_sums, 0)
    for h in range(count):
        start = 2 * ROWS * h
        moments[h] = total_ref[start : start + ROWS] + total_ref[start + ROWS : start + 2 * ROWS]

    pl.semaphore_wait(barrier, peers)
    total = sum_stage(group, moments, land_sum, send_sum, recv_sum)
    solved = solve_sources([total[r : r + 1, :] for r in range(20)])
    zero = jnp.zeros_like(solved[0])
    solved_ref[...] = jnp.concatenate(solved + [zero] * 3, axis=0)

    def place(position, block):
        span = pl.ds(pl.multiple_of(position * LOW, LOW), LOW)
        new_ref[:, span] = sources_ref[:, span] + block[:5]
        changes[position] = block

    spread_stage(group, solved_ref, land_spread, send_spread, recv_spread, place)
    table = changes[...].reshape(count * 8, LOW)
    high, low = two_parts(table)

    def use_changes(chunk, carry):
        span = pl.ds(pl.multiple_of(chunk * CHUNK, CHUNK), CHUNK)
        index = index_ref[:, span]
        owner = chosen(lax.div(index, LOW), count)
        picks = chosen(lax.rem(index, LOW), LOW).astype(jnp.bfloat16)
        found = jnp.dot(high, picks, preferred_element_type=jnp.float32)
        found = found + jnp.dot(low, picks, preferred_element_type=jnp.float32)
        picked = found[0:8] * owner[0:1]
        for h in range(1, count):
            picked = picked + found[8 * h : 8 * h + 8] * owner[h : h + 1]
        values = partials_ref[:, span].astype(jnp.float32)
        fitted = jnp.sum(values * picked[:5], axis=0, keepdims=True)
        weighted_ref[:, span] = weights_ref[:, span] * (residuals_ref[:, span] - fitted)
        return carry

    lax.fori_loop(0, chunks, use_changes, 0)


def source_updates(residuals, weights, partials, index, sources, group):
    count = group[0]
    return pl.pallas_call(
        functools.partial(source_kernel, group),
        name="source_updates",
        out_shape=(
            jax.ShapeDtypeStruct(sources.shape, jnp.float32),
            jax.ShapeDtypeStruct((1,) + residuals.shape, jnp.float32),
        ),
        in_specs=[VMEM] * 5,
        out_specs=(VMEM, VMEM),
        scratch_shapes=[
            pltpu.VMEM((count * 2 * ROWS, LOW), jnp.float32),
            pltpu.VMEM((count, ROWS, LOW), jnp.float32),
            pltpu.VMEM((8, LOW), jnp.float32),
            pltpu.VMEM((count, 8, LOW), jnp.float32),
        ]
        + stage_scratch(group, (ROWS, LOW))
        + stage_scratch(group, (8, LOW)),
        compiler_params=pltpu.CompilerParams(
            collective_id=1, has_side_effects=True, vmem_limit_bytes=48 << 20
        ),
    )(residuals[None], weights[None], partials, index[None], sources)


def applied(inverse, vector, knots):
    parts = [None] * 4
    for row in range(knots):
        term = inverse[row] * vector[row : row + 1, :]
        spot = row % 4
        parts[spot] = term if parts[spot] is None else parts[spot] + term
    return (parts[0] + parts[1]) + (parts[2] + parts[3])


def attitude_kernel(
    knots,
    count,
    blocks_ref,
    ties_ref,
    o_ref,
    inverse,
    sent,
    land,
    send_sem,
    recv_sem,
    quarters,
    corner,
    eighth,
    packed_ref,
    *stages,
):
    me = lax.axis_index("tm")
    plane, depth = along_plane(), along_depth()
    after, before = lax.rem(me + 1, count), lax.rem(me + count - 1, count)
    barrier = pltpu.get_barrier_semaphore()
    for peer in (before, after):
        pl.semaphore_signal(barrier, inc=1, device_id={"tm": peer}, device_id_type=MESH)
    peers = 2 + signal_all(barrier, plane) + signal_all(barrier, depth)
    pl.semaphore_wait(barrier, peers)

    total = sum_stage(plane, blocks_ref, *stages[0:3])
    for part in range(depth[0]):
        quarters[part] = total[PIECE * part : PIECE * (part + 1)]
    corner[...] = sum_stage(depth, quarters, *stages[3:6])

    def place_quarter(position, block):
        eighth[pl.ds(pl.multiple_of(position * PIECE, PIECE), PIECE), :] = block

    spread_stage(depth, corner, *stages[6:9], place_quarter)
    span = depth[0] * PIECE

    def place_eighth(position, block):
        packed_ref[pl.ds(pl.multiple_of(position * span, span), span), :] = block

    spread_stage(plane, eighth, *stages[9:12], place_eighth)

    left, right = ties_ref[0:1, :], ties_ref[1:2, :]
    lanes = left.shape[1]
    row_ids = lax.broadcasted_iota(jnp.int32, (knots, lanes), 0)
    start = 0
    for group in range(knots // BLOCK):
        width = (group + 1) * BLOCK
        for k in range(group * BLOCK, width):
            row = packed_ref[start : start + width, :]
            row = row + jnp.where(row_ids[:width] == k, left + right, 0.0)
            inverse[k, :width, :] = row
            start += width
    for low in range(knots // BLOCK):
        for high in range(low + 1, knots // BLOCK):
            rows = pl.ds(high * BLOCK, BLOCK)
            for k in range(low * BLOCK, (low + 1) * BLOCK):
                inverse[k, rows, :] = inverse[rows, k, :]
    right_side = packed_ref[start : start + knots, :]

    def pivot(p, carry):
        own = inverse[p]
        here = row_ids == p
        scale = 1.0 / inverse[p, pl.ds(p, 1), :]
        row = jnp.where(here, scale, own * scale)
        for i in range(knots):
            factor = inverse[i, pl.ds(p, 1), :]
            inverse[i] = jnp.where(here, 0.0, inverse[i]) - factor * row
        inverse[p] = row
        return carry

    lax.fori_loop(0, knots, pivot, 0)

    base = DAMPING * applied(inverse, right_side, knots)
    lane_ids = lax.broadcasted_iota(jnp.int32, (knots, lanes), 1)
    change = base
    for sweep in range(ITERS - 1):
        sent[sweep] = change
        copies = []
        for side, peer in enumerate((after, before)):
            copy = pltpu.make_async_remote_copy(
                src_ref=sent.at[sweep],
                dst_ref=land.at[sweep, side],
                send_sem=send_sem.at[sweep, side],
                recv_sem=recv_sem.at[sweep, side],
                device_id={"tm": peer},
                device_id_type=MESH,
            )
            copy.start()
            copies.append(copy)
        own_low, own_high = pltpu.roll(change, 1, 1), pltpu.roll(change, lanes - 1, 1)
        for copy in copies:
            copy.wait()
        low = jnp.where(lane_ids == 0, pltpu.roll(land[sweep, 0], 1, 1), own_low)
        high = jnp.where(
            lane_ids == lanes - 1, pltpu.roll(land[sweep, 1], lanes - 1, 1), own_high
        )
        tied = left * low + right * high
        change = (1.0 - DAMPING) * change + base + DAMPING * applied(inverse, tied, knots)
    o_ref[...] = change


def attitude_change(blocks, ties, knots, count):
    lanes = ties.shape[1]
    plane, depth = along_plane(), along_depth()
    whole = (depth[0] * PIECE, lanes)
    sweeps = ITERS - 1
    return pl.pallas_call(
        functools.partial(attitude_kernel, knots, count),
        name="attitude_change",
        out_shape=jax.ShapeDtypeStruct((knots, lanes), jnp.float32),
        in_specs=[VMEM, VMEM],
        out_specs=VMEM,
        scratch_shapes=[
            pltpu.VMEM((knots, knots, lanes), jnp.float32),
            pltpu.VMEM((sweeps, knots, lanes), jnp.float32),
            pltpu.VMEM((sweeps, 2, knots, lanes), jnp.float32),
            pltpu.SemaphoreType.DMA((sweeps, 2)),
            pltpu.SemaphoreType.DMA((sweeps, 2)),
            pltpu.VMEM((depth[0], PIECE, lanes), jnp.float32),
            pltpu.VMEM((PIECE, lanes), jnp.float32),
            pltpu.VMEM(whole, jnp.float32),
            pltpu.VMEM((plane[0] * whole[0], lanes), jnp.float32),
        ]
        + stage_scratch(plane, whole)
        + stage_scratch(depth, (PIECE, lanes))
        + stage_scratch(depth, (PIECE, lanes))
        + stage_scratch(plane, whole),
        compiler_params=pltpu.CompilerParams(collective_id=7, has_side_effects=True),
    )(blocks, ties)


def on_device(
    residuals,
    weights,
    source_partials,
    attitude_partials,
    source_index,
    tile_window,
    sources,
    attitude,
    coupling,
):
    window_count, knot_count = attitude.shape
    tile_count = attitude_partials.shape[1] // TILE
    times = lax.axis_size("tm")
    time_group = along_time(times)

    new_sources, weighted = source_updates(
        residuals, weights, source_partials, source_index, sources, time_group
    )

    scaled = (weights[None, :] * attitude_partials.astype(jnp.float32)).astype(jnp.bfloat16)
    shaped_att = attitude_partials.reshape(knot_count, tile_count, TILE)
    tile_normal = jnp.einsum(
        "ktp,ltp->tkl",
        scaled.reshape(knot_count, tile_count, TILE),
        shaped_att,
        preferred_element_type=jnp.float32,
    )
    tile_normal = 0.5 * (tile_normal + jnp.swapaxes(tile_normal, 1, 2))
    tile_lower = jnp.concatenate(
        [
            tile_normal[:, b : b + BLOCK, : b + BLOCK].reshape(tile_count, -1)
            for b in range(0, knot_count, BLOCK)
        ],
        axis=1,
    )

    tile_rhs = jnp.einsum(
        "ktp,tp->tk",
        shaped_att,
        weighted.astype(jnp.bfloat16).reshape(tile_count, TILE),
        preferred_element_type=jnp.float32,
    )
    tile_rows = jnp.concatenate([tile_lower, tile_rhs], axis=1)
    first_window = lax.axis_index("tm") * window_count
    window_ids = lax.broadcasted_iota(jnp.int32, (tile_count, window_count), 1)
    selector = (tile_window[:, None] - first_window == window_ids).astype(jnp.float32)
    packed = lax.dot_general(
        tile_rows, selector, (((0,), (0,)), ((), ())), precision=HIGHEST
    )
    packed = jnp.pad(packed, ((0, 768 - packed.shape[0]), (0, 0)))

    earlier = lax.ppermute(coupling[-1:], "tm", [(i, i + 1) for i in range(times - 1)])
    left = jnp.concatenate([earlier, coupling[:-1]])
    is_final = lax.axis_index("tm") == times - 1
    final_slot = lax.broadcasted_iota(jnp.int32, (window_count,), 0) == window_count - 1
    right = jnp.where(jnp.logical_and(is_final, final_slot), 0.0, coupling)
    change = attitude_change(
        packed.reshape(8, 4 * PIECE, window_count), jnp.stack([left, right]), knot_count, times
    )
    return (new_sources, attitude + change.T)


def solution(mesh):
    return jax.shard_map(
        on_device,
        mesh=mesh,
        in_specs=(
            P(("sky", "tm")),
            P(("sky", "tm")),
            P(None, ("sky", "tm")),
            P(None, ("sky", "tm")),
            P(("sky", "tm")),
            P(("sky", "tm")),
            P(None, "sky"),
            P("tm", None),
            P("tm"),
        ),
        out_specs=(P(None, "sky"), P("tm", None)),
        check_vma=False,
    )
```

```python
import functools

import jax
import jax.numpy as jnp
from jax import lax
from jax.experimental import pallas as pl
from jax.experimental.pallas import tpu as pltpu
from jax.sharding import PartitionSpec as P

TILE = 128
ITERS = 8
BLOCK = 8
PIECE = 24
LOWER_PAIRS = tuple(((i, j) for i in range(5) for j in range(i + 1)))
DAMPING = 0.8
HIGHEST = lax.Precision.HIGHEST
MESH = pl.DeviceIdType.MESH
VMEM = pl.BlockSpec(memory_space=pltpu.VMEM)


def along_time(count):
    return count, lambda: lax.axis_index("tm"), lambda p: {"tm": p}


def along_plane():
    def spot():
        sky = lax.axis_index("sky")
        return lax.div(sky, 8) * 2 + lax.rem(sky, 2)

    def name(p):
        depth = lax.rem(lax.div(lax.axis_index("sky"), 2), 4)
        return {"sky": lax.div(p, 2) * 8 + depth * 2 + lax.rem(p, 2)}

    return 8, spot, name


def along_depth():
    def spot():
        return lax.rem(lax.div(lax.axis_index("sky"), 2), 4)

    def name(p):
        sky = lax.axis_index("sky")
        return {"sky": lax.div(sky, 8) * 8 + p * 2 + lax.rem(sky, 2)}

    return 4, spot, name


def signal_all(barrier, group):
    count, spot, name = group
    me = spot()
    for step in range(1, count):
        peer = lax.rem(me + step, count)
        pl.semaphore_signal(barrier, inc=1, device_id=name(peer), device_id_type=MESH)
    return count - 1


def send_all(group, source, land, send_sem, recv_sem):
    count, spot, name = group
    me = spot()
    copies = []
    for step in range(1, count):
        peer = lax.rem(me + step, count)
        copy = pltpu.make_async_remote_copy(
            src_ref=source(peer),
            dst_ref=land.at[step - 1],
            send_sem=send_sem.at[step - 1],
            recv_sem=recv_sem.at[step - 1],
            device_id=name(peer),
            device_id_type=MESH,
        )
        copy.start()
        copies.append(copy)
    return copies


def finish_sends(copies):
    for copy in copies:
        copy.wait_send()


def finish_sum(group, copies, x_ref, land):
    total = x_ref[group[1]()]
    for step, copy in enumerate(copies):
        copy.wait_recv()
        total = total + land[step]
    finish_sends(copies)
    return total


def finish_spread(group, copies, x_ref, land, place):
    count, spot, _ = group
    me = spot()
    place(me, x_ref[...])
    for step, copy in enumerate(copies):
        copy.wait_recv()
        place(lax.rem(me + count - step - 1, count), land[step])
    finish_sends(copies)


def start_sum(group, x_ref, stage):
    return send_all(group, lambda peer: x_ref.at[peer], *stage)


def start_spread(group, x_ref, stage):
    return send_all(group, lambda peer: x_ref, *stage)


def finish_ordered(group, copies, x_ref, land, held):
    def place(position, block):
        held[position] = block

    finish_spread(group, copies, x_ref, land, place)
    total = held[0]
    for position in range(1, group[0]):
        total = total + held[position]
    return total


def stage_scratch(group, block):
    peers = group[0] - 1
    return [
        pltpu.VMEM((peers,) + block, jnp.float32),
        pltpu.SemaphoreType.DMA((peers,)),
        pltpu.SemaphoreType.DMA((peers,)),
    ]


def solve_sources(moments):
    matrix = {}
    for position, pair in enumerate(LOWER_PAIRS):
        matrix[pair] = moments[position] + (1.0 if pair[0] == pair[1] else 0.0)
    factor = {}
    for i in range(5):
        for j in range(i + 1):
            reduced = matrix[i, j]
            for k in range(j):
                reduced = reduced - factor[i, k] * factor[j, k]
            if i == j:
                factor[i, i] = jnp.sqrt(reduced)
            else:
                factor[i, j] = reduced / factor[j, j]
    forward = []
    for i in range(5):
        current = moments[15 + i]
        for k in range(i):
            current = current - factor[i, k] * forward[k]
        forward.append(current / factor[i, i])
    result = [None] * 5
    for i in reversed(range(5)):
        current = forward[i]
        for k in range(i + 1, 5):
            current = current - factor[k, i] * result[k]
        result[i] = current / factor[i, i]
    return result


CHUNK = 1024
LOW = 256
ROWS = 24


def two_parts(values):
    high = values.astype(jnp.bfloat16)
    return high, (values - high.astype(jnp.float32)).astype(jnp.bfloat16)


def chosen(index, count):
    ids = lax.broadcasted_iota(jnp.int32, (count, index.shape[1]), 0)
    return (ids == index).astype(jnp.float32)


def applied(inverse, vector, knots):
    parts = [None] * 4
    for row in range(knots):
        term = inverse[row] * vector[row : row + 1, :]
        spot = row % 4
        parts[spot] = term if parts[spot] is None else parts[spot] + term
    return (parts[0] + parts[1]) + (parts[2] + parts[3])


def update_kernel(
    knots,
    group,
    residuals_ref,
    weights_ref,
    partials_ref,
    index_ref,
    sources_ref,
    blocks_ref,
    ties_ref,
    attitude_ref,
    window_ref,
    new_ref,
    o_ref,
    total_ref,
    moments,
    solved_ref,
    changes,
    quarters,
    corner,
    eighth,
    packed_ref,
    rhs_ref,
    rhs_part,
    rhs_plane,
    rhs_depth,
    inverse,
    sent,
    land,
    send_sem,
    recv_sem,
    *scratch,
):
    stages = [scratch[i : i + 3] for i in range(0, len(scratch), 3)]
    plane, depth = along_plane(), along_depth()
    count = group[0]
    barrier = pltpu.get_barrier_semaphore()
    peers = signal_all(barrier, group) + signal_all(barrier, plane) + signal_all(barrier, depth)
    chunks = residuals_ref.shape[1] // CHUNK
    total_ref[...] = jnp.zeros_like(total_ref)

    def gather_sums(chunk, carry):
        span = pl.ds(pl.multiple_of(chunk * CHUNK, CHUNK), CHUNK)
        index = index_ref[:, span]
        weights = weights_ref[:, span]
        residuals = residuals_ref[:, span]
        values = partials_ref[:, span].astype(jnp.float32)
        rows = [values[i : i + 1, :] for i in range(5)]
        scaled = [weights * row for row in rows]
        entries = [scaled[i] * rows[j] for i, j in LOWER_PAIRS]
        entries = entries + [scaled[i] * residuals for i in range(5)]
        entries = entries + [jnp.zeros_like(weights)] * (ROWS - 20)
        high, low = two_parts(jnp.concatenate(entries, axis=0))
        both = jnp.concatenate([high, low], axis=0)
        owner = chosen(lax.div(index, LOW), count)
        held = [both * owner[h : h + 1, :].astype(jnp.bfloat16) for h in range(count)]
        held = jnp.concatenate(held, axis=0)
        picks = chosen(lax.rem(index, LOW), LOW).astype(jnp.bfloat16)
        total_ref[...] += lax.dot_general(
            held, picks, (((1,), (1,)), ((), ())), preferred_element_type=jnp.float32
        )
        return carry

    lax.fori_loop(0, chunks, gather_sums, 0)
    for h in range(count):
        start = 2 * ROWS * h
        moments[h] = total_ref[start : start + ROWS] + total_ref[start + ROWS : start + 2 * ROWS]

    pl.semaphore_wait(barrier, peers)
    plane_sum = start_sum(plane, blocks_ref, stages[2])
    time_sum = start_sum(group, moments, stages[0])

    total = finish_sum(plane, plane_sum, blocks_ref, stages[2][0])
    for part in range(depth[0]):
        quarters[part] = total[PIECE * part : PIECE * (part + 1)]
    depth_sum = start_sum(depth, quarters, stages[3])

    total = finish_sum(group, time_sum, moments, stages[0][0])
    solved = solve_sources([total[r : r + 1, :] for r in range(20)])
    zero = jnp.zeros_like(solved[0])
    solved_ref[...] = jnp.concatenate(solved + [zero] * 3, axis=0)
    time_spread = start_spread(group, solved_ref, stages[1])

    corner[...] = finish_sum(depth, depth_sum, quarters, stages[3][0])
    depth_spread = start_spread(depth, corner, stages[4])

    def place(position, block):
        span = pl.ds(pl.multiple_of(position * LOW, LOW), LOW)
        new_ref[:, span] = sources_ref[:, span] + block[:5]
        changes[position] = block

    finish_spread(group, time_spread, solved_ref, stages[1][0], place)
    table = changes[...].reshape(count * 8, LOW)
    high, low = two_parts(table)

    def use_changes(chunk, carry):
        span = pl.ds(pl.multiple_of(chunk * CHUNK, CHUNK), CHUNK)
        index = index_ref[:, span]
        owner = chosen(lax.div(index, LOW), count)
        picks = chosen(lax.rem(index, LOW), LOW).astype(jnp.bfloat16)
        found = jnp.dot(high, picks, preferred_element_type=jnp.float32)
        found = found + jnp.dot(low, picks, preferred_element_type=jnp.float32)
        picked = found[0:8] * owner[0:1]
        for h in range(1, count):
            picked = picked + found[8 * h : 8 * h + 8] * owner[h : h + 1]
        values = partials_ref[:, span].astype(jnp.float32)
        fitted = jnp.sum(values * picked[:5], axis=0, keepdims=True)
        weighted = weights_ref[:, span] * (residuals_ref[:, span] - fitted)
        tied = chosen(window_ref[:, span], lanes) * weighted.astype(jnp.bfloat16).astype(jnp.float32)
        rhs_ref[...] += lax.dot_general(
            attitude_ref[:, span],
            tied.astype(jnp.bfloat16),
            (((1,), (1,)), ((), ())),
            preferred_element_type=jnp.float32,
        )
        return carry

    lanes = ties_ref.shape[1]
    rhs_ref[...] = jnp.zeros_like(rhs_ref)
    lax.fori_loop(0, chunks, use_changes, 0)
    rhs_first = start_spread(plane, rhs_ref, stages[6])

    def place_quarter(position, block):
        eighth[pl.ds(pl.multiple_of(position * PIECE, PIECE), PIECE), :] = block

    finish_spread(depth, depth_spread, corner, stages[4][0], place_quarter)
    plane_spread = start_spread(plane, eighth, stages[5])
    rhs_part[...] = finish_ordered(plane, rhs_first, rhs_ref, stages[6][0], rhs_plane)
    rhs_second = start_spread(depth, rhs_part, stages[7])
    width = depth[0] * PIECE

    def place_eighth(position, block):
        packed_ref[pl.ds(pl.multiple_of(position * width, width), width), :] = block

    finish_spread(plane, plane_spread, eighth, stages[5][0], place_eighth)

    left, right = ties_ref[0:1, :], ties_ref[1:2, :]
    row_ids = lax.broadcasted_iota(jnp.int32, (knots, lanes), 0)
    start = 0
    for group in range(knots // BLOCK):
        width = (group + 1) * BLOCK
        for k in range(group * BLOCK, width):
            row = packed_ref[start : start + width, :]
            row = row + jnp.where(row_ids[:width] == k, left + right, 0.0)
            inverse[k, :width, :] = row
            start += width
    for low in range(knots // BLOCK):
        for high in range(low + 1, knots // BLOCK):
            rows = pl.ds(high * BLOCK, BLOCK)
            for k in range(low * BLOCK, (low + 1) * BLOCK):
                inverse[k, rows, :] = inverse[rows, k, :]

    def pivot(p, carry):
        own = inverse[p]
        here = row_ids == p
        scale = 1.0 / inverse[p, pl.ds(p, 1), :]
        row = jnp.where(here, scale, own * scale)
        factors = jnp.where(row_ids < p, -own, own)
        for i in range(knots):
            inverse[i] = jnp.where(here, 0.0, inverse[i]) - factors[i : i + 1, :] * row
        inverse[p] = row
        return carry

    lax.fori_loop(0, knots, pivot, 0)

    right_side = finish_ordered(depth, rhs_second, rhs_part, stages[7][0], rhs_depth)
    base = DAMPING * applied(inverse, right_side, knots)
    lane_ids = lax.broadcasted_iota(jnp.int32, (knots, lanes), 1)
    first, last = lane_ids == 0, lane_ids == lanes - 1
    me = lax.axis_index("tm")
    has_before, has_after = me > 0, me < count - 1
    after, before = lax.rem(me + 1, count), lax.rem(me + count - 1, count)
    change = base
    for sweep in range(ITERS - 1):
        sent[sweep] = change
        ahead, behind = [
            pltpu.make_async_remote_copy(
                src_ref=sent.at[sweep],
                dst_ref=land.at[sweep, side],
                send_sem=send_sem.at[sweep, side],
                recv_sem=recv_sem.at[sweep, side],
                device_id={"tm": peer},
                device_id_type=MESH,
            )
            for side, peer in enumerate((after, before))
        ]
        pl.when(has_after)(ahead.start)
        pl.when(has_before)(behind.start)
        own_low = jnp.where(first, 0.0, pltpu.roll(change, 1, 1))
        own_high = jnp.where(last, 0.0, pltpu.roll(change, lanes - 1, 1))
        pl.when(has_before)(ahead.wait_recv)
        pl.when(has_after)(behind.wait_recv)
        low, high = pltpu.roll(land[sweep, 0], 1, 1), pltpu.roll(land[sweep, 1], lanes - 1, 1)
        low = jnp.where(jnp.logical_and(first, has_before), low, own_low)
        high = jnp.where(jnp.logical_and(last, has_after), high, own_high)
        tied = left * low + right * high
        change = (1.0 - DAMPING) * change + base + DAMPING * applied(inverse, tied, knots)
        pl.when(has_after)(ahead.wait_send)
        pl.when(has_before)(behind.wait_send)
    o_ref[...] = change


def updates(residuals, weights, partials, index, sources, blocks, ties, attitude, window, group):
    knots, lanes, count = attitude.shape[0], ties.shape[1], group[0]
    sweeps = ITERS - 1
    plane, depth = along_plane(), along_depth()
    piece, whole, side = (PIECE, lanes), (depth[0] * PIECE, lanes), (knots, lanes)

    def held(*shape):
        return pltpu.VMEM(shape, jnp.float32)

    return pl.pallas_call(
        functools.partial(update_kernel, knots, group),
        name="updates",
        out_shape=(
            jax.ShapeDtypeStruct(sources.shape, jnp.float32),
            jax.ShapeDtypeStruct(side, jnp.float32),
        ),
        in_specs=[VMEM] * 9,
        out_specs=(VMEM, VMEM),
        scratch_shapes=[
            held(count * 2 * ROWS, LOW),
            held(count, ROWS, LOW),
            held(8, LOW),
            held(count, 8, LOW),
            held(depth[0], *piece),
            held(*piece),
            held(*whole),
            held(plane[0] * whole[0], lanes),
            held(*side),
            held(*side),
            held(plane[0], *side),
            held(depth[0], *side),
            held(knots, *side),
            held(sweeps, *side),
            held(sweeps, 2, *side),
            pltpu.SemaphoreType.DMA((sweeps, 2)),
            pltpu.SemaphoreType.DMA((sweeps, 2)),
        ]
        + stage_scratch(group, (ROWS, LOW))
        + stage_scratch(group, (8, LOW))
        + stage_scratch(plane, whole)
        + stage_scratch(depth, piece)
        + stage_scratch(depth, piece)
        + stage_scratch(plane, whole)
        + stage_scratch(plane, side)
        + stage_scratch(depth, side),
        compiler_params=pltpu.CompilerParams(
            collective_id=1, has_side_effects=True, vmem_limit_bytes=48 << 20
        ),
    )(residuals[None], weights[None], partials, index[None], sources, blocks, ties, attitude, window[None])


def on_device(
    residuals,
    weights,
    source_partials,
    attitude_partials,
    source_index,
    tile_window,
    sources,
    attitude,
    coupling,
):
    window_count, knot_count = attitude.shape
    tile_count = attitude_partials.shape[1] // TILE
    times = lax.axis_size("tm")
    time_group = along_time(times)

    scaled = (weights[None, :] * attitude_partials.astype(jnp.float32)).astype(jnp.bfloat16)
    shaped_att = attitude_partials.reshape(knot_count, tile_count, TILE)
    tile_normal = jnp.einsum(
        "ktp,ltp->tkl",
        scaled.reshape(knot_count, tile_count, TILE),
        shaped_att,
        preferred_element_type=jnp.float32,
    )
    tile_normal = 0.5 * (tile_normal + jnp.swapaxes(tile_normal, 1, 2))
    tile_lower = jnp.concatenate(
        [
            tile_normal[:, b : b + BLOCK, : b + BLOCK].reshape(tile_count, -1)
            for b in range(0, knot_count, BLOCK)
        ],
        axis=1,
    )

    first_window = lax.axis_index("tm") * window_count
    window_ids = lax.broadcasted_iota(jnp.int32, (tile_count, window_count), 1)
    selector = (tile_window[:, None] - first_window == window_ids).astype(jnp.float32)
    packed = lax.dot_general(
        tile_lower, selector, (((0,), (0,)), ((), ())), precision=HIGHEST
    )
    packed = jnp.pad(packed, ((0, 768 - packed.shape[0]), (0, 0)))

    earlier = lax.ppermute(coupling[-1:], "tm", [(i, i + 1) for i in range(times - 1)])
    left = jnp.concatenate([earlier, coupling[:-1]])
    is_final = lax.axis_index("tm") == times - 1
    final_slot = lax.broadcasted_iota(jnp.int32, (window_count,), 0) == window_count - 1
    right = jnp.where(jnp.logical_and(is_final, final_slot), 0.0, coupling)
    new_sources, change = updates(
        residuals,
        weights,
        source_partials,
        source_index,
        sources,
        packed.reshape(8, 4 * PIECE, window_count),
        jnp.stack([left, right]),
        attitude_partials,
        jnp.repeat(tile_window - first_window, TILE, total_repeat_length=residuals.shape[0]),
        time_group,
    )
    return (new_sources, attitude + change.T)


def solution(mesh):
    return jax.shard_map(
        on_device,
        mesh=mesh,
        in_specs=(
            P(("sky", "tm")),
            P(("sky", "tm")),
            P(None, ("sky", "tm")),
            P(None, ("sky", "tm")),
            P(("sky", "tm")),
            P(("sky", "tm")),
            P(None, "sky"),
            P("tm", None),
            P("tm"),
        ),
        out_specs=(P(None, "sky"), P("tm", None)),
        check_vma=False,
    )
```

```python
import functools

import jax
import jax.numpy as jnp
from jax import lax
from jax.experimental import pallas as pl
from jax.experimental.pallas import tpu as pltpu
from jax.sharding import PartitionSpec as P

TILE = 128
ITERS = 8
BLOCK = 8
PIECE = 24
LOWER_PAIRS = tuple(((i, j) for i in range(5) for j in range(i + 1)))
DAMPING = 0.8
HIGHEST = lax.Precision.HIGHEST
MESH = pl.DeviceIdType.MESH
VMEM = pl.BlockSpec(memory_space=pltpu.VMEM)


def along_time(count):
    return count, lambda: lax.axis_index("tm"), lambda p: {"tm": p}


def along_plane():
    def spot():
        sky = lax.axis_index("sky")
        return lax.div(sky, 8) * 2 + lax.rem(sky, 2)

    def name(p):
        depth = lax.rem(lax.div(lax.axis_index("sky"), 2), 4)
        return {"sky": lax.div(p, 2) * 8 + depth * 2 + lax.rem(p, 2)}

    return 8, spot, name


def along_depth():
    def spot():
        return lax.rem(lax.div(lax.axis_index("sky"), 2), 4)

    def name(p):
        sky = lax.axis_index("sky")
        return {"sky": lax.div(sky, 8) * 8 + p * 2 + lax.rem(sky, 2)}

    return 4, spot, name


def signal_all(barrier, group):
    count, spot, name = group
    me = spot()
    for step in range(1, count):
        peer = lax.rem(me + step, count)
        pl.semaphore_signal(barrier, inc=1, device_id=name(peer), device_id_type=MESH)
    return count - 1


def send_all(group, source, land, send_sem, recv_sem):
    count, spot, name = group
    me = spot()
    copies = []
    for step in range(1, count):
        peer = lax.rem(me + step, count)
        copy = pltpu.make_async_remote_copy(
            src_ref=source(peer),
            dst_ref=land.at[step - 1],
            send_sem=send_sem.at[step - 1],
            recv_sem=recv_sem.at[step - 1],
            device_id=name(peer),
            device_id_type=MESH,
        )
        copy.start()
        copies.append(copy)
    return copies


def finish_sends(copies):
    for copy in copies:
        copy.wait_send()


def finish_sum(group, copies, x_ref, land):
    total = x_ref[group[1]()]
    for step, copy in enumerate(copies):
        copy.wait_recv()
        total = total + land[step]
    finish_sends(copies)
    return total


def finish_spread(group, copies, x_ref, land, place):
    count, spot, _ = group
    me = spot()
    place(me, x_ref[...])
    for step, copy in enumerate(copies):
        copy.wait_recv()
        place(lax.rem(me + count - step - 1, count), land[step])
    finish_sends(copies)


def start_sum(group, x_ref, stage):
    return send_all(group, lambda peer: x_ref.at[peer], *stage)


def start_spread(group, x_ref, stage):
    return send_all(group, lambda peer: x_ref, *stage)


def finish_ordered(group, copies, x_ref, land, held):
    def place(position, block):
        held[position] = block

    finish_spread(group, copies, x_ref, land, place)
    total = held[0]
    for position in range(1, group[0]):
        total = total + held[position]
    return total


def stage_scratch(group, block):
    peers = group[0] - 1
    return [
        pltpu.VMEM((peers,) + block, jnp.float32),
        pltpu.SemaphoreType.DMA((peers,)),
        pltpu.SemaphoreType.DMA((peers,)),
    ]


def solve_sources(moments):
    matrix = {}
    for position, pair in enumerate(LOWER_PAIRS):
        matrix[pair] = moments[position] + (1.0 if pair[0] == pair[1] else 0.0)
    factor = {}
    for i in range(5):
        for j in range(i + 1):
            reduced = matrix[i, j]
            for k in range(j):
                reduced = reduced - factor[i, k] * factor[j, k]
            if i == j:
                factor[i, i] = jnp.sqrt(reduced)
            else:
                factor[i, j] = reduced / factor[j, j]
    forward = []
    for i in range(5):
        current = moments[15 + i]
        for k in range(i):
            current = current - factor[i, k] * forward[k]
        forward.append(current / factor[i, i])
    result = [None] * 5
    for i in reversed(range(5)):
        current = forward[i]
        for k in range(i + 1, 5):
            current = current - factor[k, i] * result[k]
        result[i] = current / factor[i, i]
    return result


CHUNK = 1024
LOW = 256
ROWS = 24


def two_parts(values):
    high = values.astype(jnp.bfloat16)
    return high, (values - high.astype(jnp.float32)).astype(jnp.bfloat16)


def chosen(index, count):
    ids = lax.broadcasted_iota(jnp.int32, (count, index.shape[1]), 0)
    return (ids == index).astype(jnp.float32)


def applied(inverse, vector, knots):
    parts = [None] * 4
    for row in range(knots):
        term = inverse[row] * vector[row : row + 1, :]
        spot = row % 4
        parts[spot] = term if parts[spot] is None else parts[spot] + term
    return (parts[0] + parts[1]) + (parts[2] + parts[3])


def update_kernel(
    knots,
    group,
    residuals_ref,
    weights_ref,
    partials_ref,
    index_ref,
    sources_ref,
    blocks_ref,
    ties_ref,
    attitude_ref,
    window_ref,
    new_ref,
    o_ref,
    total_ref,
    moments,
    solved_ref,
    changes,
    quarters,
    corner,
    eighth,
    packed_ref,
    rhs_ref,
    rhs_part,
    rhs_plane,
    rhs_depth,
    inverse,
    sent,
    land,
    send_sem,
    recv_sem,
    *scratch,
):
    stages = [scratch[i : i + 3] for i in range(0, len(scratch), 3)]
    plane, depth = along_plane(), along_depth()
    count = group[0]
    barrier = pltpu.get_barrier_semaphore()
    peers = signal_all(barrier, group) + signal_all(barrier, plane) + signal_all(barrier, depth)
    chunks = residuals_ref.shape[1] // CHUNK
    total_ref[...] = jnp.zeros_like(total_ref)

    def gather_sums(chunk, carry):
        span = pl.ds(pl.multiple_of(chunk * CHUNK, CHUNK), CHUNK)
        index = index_ref[:, span]
        weights = weights_ref[:, span]
        residuals = residuals_ref[:, span]
        values = partials_ref[:, span].astype(jnp.float32)
        rows = [values[i : i + 1, :] for i in range(5)]
        scaled = [weights * row for row in rows]
        entries = [scaled[i] * rows[j] for i, j in LOWER_PAIRS]
        entries = entries + [scaled[i] * residuals for i in range(5)]
        entries = entries + [jnp.zeros_like(weights)] * (ROWS - 20)
        high, low = two_parts(jnp.concatenate(entries, axis=0))
        both = jnp.concatenate([high, low], axis=0)
        owner = chosen(lax.div(index, LOW), count)
        held = [both * owner[h : h + 1, :].astype(jnp.bfloat16) for h in range(count)]
        held = jnp.concatenate(held, axis=0)
        picks = chosen(lax.rem(index, LOW), LOW).astype(jnp.bfloat16)
        total_ref[...] += lax.dot_general(
            held, picks, (((1,), (1,)), ((), ())), preferred_element_type=jnp.float32
        )
        return carry

    lax.fori_loop(0, chunks, gather_sums, 0)
    for h in range(count):
        start = 2 * ROWS * h
        moments[h] = total_ref[start : start + ROWS] + total_ref[start + ROWS : start + 2 * ROWS]

    pl.semaphore_wait(barrier, peers)
    plane_sum = start_sum(plane, blocks_ref, stages[2])
    time_sum = start_sum(group, moments, stages[0])

    total = finish_sum(plane, plane_sum, blocks_ref, stages[2][0])
    for part in range(depth[0]):
        quarters[part] = total[PIECE * part : PIECE * (part + 1)]
    depth_sum = start_sum(depth, quarters, stages[3])

    total = finish_sum(group, time_sum, moments, stages[0][0])
    solved = solve_sources([total[r : r + 1, :] for r in range(20)])
    zero = jnp.zeros_like(solved[0])
    solved_ref[...] = jnp.concatenate(solved + [zero] * 3, axis=0)
    time_spread = start_spread(group, solved_ref, stages[1])

    corner[...] = finish_sum(depth, depth_sum, quarters, stages[3][0])
    depth_spread = start_spread(depth, corner, stages[4])

    def place(position, block):
        span = pl.ds(pl.multiple_of(position * LOW, LOW), LOW)
        new_ref[:, span] = sources_ref[:, span] + block[:5]
        changes[position] = block

    finish_spread(group, time_spread, solved_ref, stages[1][0], place)
    table = changes[...].reshape(count * 8, LOW)
    high, low = two_parts(table)

    def use_changes(chunk, carry):
        span = pl.ds(pl.multiple_of(chunk * CHUNK, CHUNK), CHUNK)
        index = index_ref[:, span]
        owner = chosen(lax.div(index, LOW), count)
        picks = chosen(lax.rem(index, LOW), LOW).astype(jnp.bfloat16)
        found = jnp.dot(high, picks, preferred_element_type=jnp.float32)
        found = found + jnp.dot(low, picks, preferred_element_type=jnp.float32)
        picked = found[0:8] * owner[0:1]
        for h in range(1, count):
            picked = picked + found[8 * h : 8 * h + 8] * owner[h : h + 1]
        values = partials_ref[:, span].astype(jnp.float32)
        fitted = jnp.sum(values * picked[:5], axis=0, keepdims=True)
        weighted = weights_ref[:, span] * (residuals_ref[:, span] - fitted)
        tied = chosen(window_ref[:, span], lanes) * weighted.astype(jnp.bfloat16).astype(jnp.float32)
        rhs_ref[...] += lax.dot_general(
            attitude_ref[:, span],
            tied.astype(jnp.bfloat16),
            (((1,), (1,)), ((), ())),
            preferred_element_type=jnp.float32,
        )
        return carry

    lanes = ties_ref.shape[1]
    rhs_ref[...] = jnp.zeros_like(rhs_ref)
    lax.fori_loop(0, chunks, use_changes, 0)
    rhs_first = start_spread(plane, rhs_ref, stages[6])

    def place_quarter(position, block):
        eighth[pl.ds(pl.multiple_of(position * PIECE, PIECE), PIECE), :] = block

    finish_spread(depth, depth_spread, corner, stages[4][0], place_quarter)
    plane_spread = start_spread(plane, eighth, stages[5])
    rhs_part[...] = finish_ordered(plane, rhs_first, rhs_ref, stages[6][0], rhs_plane)
    rhs_second = start_spread(depth, rhs_part, stages[7])
    width = depth[0] * PIECE

    def place_eighth(position, block):
        packed_ref[pl.ds(pl.multiple_of(position * width, width), width), :] = block

    finish_spread(plane, plane_spread, eighth, stages[5][0], place_eighth)

    left, right = ties_ref[0:1, :], ties_ref[1:2, :]
    row_ids = lax.broadcasted_iota(jnp.int32, (knots, lanes), 0)
    start = 0
    for group in range(knots // BLOCK):
        width = (group + 1) * BLOCK
        for k in range(group * BLOCK, width):
            row = packed_ref[start : start + width, :]
            row = row + jnp.where(row_ids[:width] == k, left + right, 0.0)
            inverse[k, :width, :] = row
            start += width
    for low in range(knots // BLOCK):
        for high in range(low + 1, knots // BLOCK):
            rows = pl.ds(high * BLOCK, BLOCK)
            for k in range(low * BLOCK, (low + 1) * BLOCK):
                inverse[k, rows, :] = inverse[rows, k, :]

    def pivot(p, carry):
        own = inverse[p]
        here = row_ids == p
        scale = 1.0 / inverse[p, pl.ds(p, 1), :]
        row = jnp.where(here, scale, own * scale)
        factors = jnp.where(row_ids < p, -own, own)
        for i in range(knots):
            inverse[i] = jnp.where(here, 0.0, inverse[i]) - factors[i : i + 1, :] * row
        inverse[p] = row
        return carry

    lax.fori_loop(0, knots, pivot, 0)

    right_side = finish_ordered(depth, rhs_second, rhs_part, stages[7][0], rhs_depth)
    base = DAMPING * applied(inverse, right_side, knots)
    lane_ids = lax.broadcasted_iota(jnp.int32, (knots, lanes), 1)
    first, last = lane_ids == 0, lane_ids == lanes - 1
    me = lax.axis_index("tm")
    has_before, has_after = me > 0, me < count - 1
    after, before = lax.rem(me + 1, count), lax.rem(me + count - 1, count)
    change = base
    for sweep in range(ITERS - 1):
        sent[sweep] = change
        ahead, behind = [
            pltpu.make_async_remote_copy(
                src_ref=sent.at[sweep],
                dst_ref=land.at[sweep, side],
                send_sem=send_sem.at[sweep, side],
                recv_sem=recv_sem.at[sweep, side],
                device_id={"tm": peer},
                device_id_type=MESH,
            )
            for side, peer in enumerate((after, before))
        ]
        pl.when(has_after)(ahead.start)
        pl.when(has_before)(behind.start)
        own_low = jnp.where(first, 0.0, pltpu.roll(change, 1, 1))
        own_high = jnp.where(last, 0.0, pltpu.roll(change, lanes - 1, 1))
        pl.when(has_before)(ahead.wait_recv)
        pl.when(has_after)(behind.wait_recv)
        low, high = pltpu.roll(land[sweep, 0], 1, 1), pltpu.roll(land[sweep, 1], lanes - 1, 1)
        low = jnp.where(jnp.logical_and(first, has_before), low, own_low)
        high = jnp.where(jnp.logical_and(last, has_after), high, own_high)
        tied = left * low + right * high
        change = (1.0 - DAMPING) * change + base + DAMPING * applied(inverse, tied, knots)
        pl.when(has_after)(ahead.wait_send)
        pl.when(has_before)(behind.wait_send)
    o_ref[...] = change


def updates(residuals, weights, partials, index, sources, blocks, ties, attitude, window, group):
    knots, lanes, count = attitude.shape[0], ties.shape[1], group[0]
    sweeps = ITERS - 1
    plane, depth = along_plane(), along_depth()
    piece, whole, side = (PIECE, lanes), (depth[0] * PIECE, lanes), (knots, lanes)

    def held(*shape):
        return pltpu.VMEM(shape, jnp.float32)

    return pl.pallas_call(
        functools.partial(update_kernel, knots, group),
        name="updates",
        out_shape=(
            jax.ShapeDtypeStruct(sources.shape, jnp.float32),
            jax.ShapeDtypeStruct(side, jnp.float32),
        ),
        in_specs=[VMEM] * 9,
        out_specs=(VMEM, VMEM),
        scratch_shapes=[
            held(count * 2 * ROWS, LOW),
            held(count, ROWS, LOW),
            held(8, LOW),
            held(count, 8, LOW),
            held(depth[0], *piece),
            held(*piece),
            held(*whole),
            held(plane[0] * whole[0], lanes),
            held(*side),
            held(*side),
            held(plane[0], *side),
            held(depth[0], *side),
            held(knots, *side),
            held(sweeps, *side),
            held(sweeps, 2, *side),
            pltpu.SemaphoreType.DMA((sweeps, 2)),
            pltpu.SemaphoreType.DMA((sweeps, 2)),
        ]
        + stage_scratch(group, (ROWS, LOW))
        + stage_scratch(group, (8, LOW))
        + stage_scratch(plane, whole)
        + stage_scratch(depth, piece)
        + stage_scratch(depth, piece)
        + stage_scratch(plane, whole)
        + stage_scratch(plane, side)
        + stage_scratch(depth, side),
        compiler_params=pltpu.CompilerParams(
            collective_id=1, has_side_effects=True, vmem_limit_bytes=48 << 20
        ),
    )(residuals[None], weights[None], partials, index[None], sources, blocks, ties, attitude, window[None])


def on_device(
    residuals,
    weights,
    source_partials,
    attitude_partials,
    source_index,
    tile_window,
    sources,
    attitude,
    coupling,
):
    window_count, knot_count = attitude.shape
    tile_count = attitude_partials.shape[1] // TILE
    times = lax.axis_size("tm")
    time_group = along_time(times)

    scaled = (weights[None, :] * attitude_partials.astype(jnp.float32)).astype(jnp.bfloat16)
    shaped_att = attitude_partials.reshape(knot_count, tile_count, TILE)
    tile_normal = jnp.einsum(
        "ktp,ltp->tkl",
        scaled.reshape(knot_count, tile_count, TILE),
        shaped_att,
        preferred_element_type=jnp.float32,
    )
    tile_normal = 0.5 * (tile_normal + jnp.swapaxes(tile_normal, 1, 2))
    tile_lower = jnp.concatenate(
        [
            tile_normal[:, b : b + BLOCK, : b + BLOCK].reshape(tile_count, -1)
            for b in range(0, knot_count, BLOCK)
        ],
        axis=1,
    )

    first_window = lax.axis_index("tm") * window_count
    window_ids = lax.broadcasted_iota(jnp.int32, (tile_count, window_count), 1)
    selector = (tile_window[:, None] - first_window == window_ids).astype(jnp.float32)
    packed = lax.dot_general(
        tile_lower, selector, (((0,), (0,)), ((), ())), precision=HIGHEST
    )
    packed = jnp.pad(packed, ((0, 768 - packed.shape[0]), (0, 0)))

    earlier = lax.ppermute(coupling[-1:], "tm", [(i, i + 1) for i in range(times - 1)])
    left = jnp.concatenate([earlier, coupling[:-1]])
    is_final = lax.axis_index("tm") == times - 1
    final_slot = lax.broadcasted_iota(jnp.int32, (window_count,), 0) == window_count - 1
    right = jnp.where(jnp.logical_and(is_final, final_slot), 0.0, coupling)
    new_sources, change = updates(
        residuals,
        weights,
        source_partials,
        source_index,
        sources,
        packed.reshape(8, 4 * PIECE, window_count),
        jnp.stack([left, right]),
        attitude_partials,
        jnp.broadcast_to((tile_window - first_window)[:, None], (tile_count, TILE)).reshape(-1),
        time_group,
    )
    return (new_sources, attitude + change.T)


def solution(mesh):
    return jax.shard_map(
        on_device,
        mesh=mesh,
        in_specs=(
            P(("sky", "tm")),
            P(("sky", "tm")),
            P(None, ("sky", "tm")),
            P(None, ("sky", "tm")),
            P(("sky", "tm")),
            P(("sky", "tm")),
            P(None, "sky"),
            P("tm", None),
            P("tm"),
        ),
        out_specs=(P(None, "sky"), P("tm", None)),
        check_vma=False,
    )
```

```python
import functools

import jax
import jax.numpy as jnp
from jax import lax
from jax.experimental import pallas as pl
from jax.experimental.pallas import tpu as pltpu
from jax.sharding import PartitionSpec as P

TILE = 128
ITERS = 8
BLOCK = 8
PIECE = 24
LOWER_PAIRS = tuple(((i, j) for i in range(5) for j in range(i + 1)))
DAMPING = 0.8
HIGHEST = lax.Precision.HIGHEST
MESH = pl.DeviceIdType.MESH
VMEM = pl.BlockSpec(memory_space=pltpu.VMEM)


def along_time(count):
    return count, lambda: lax.axis_index("tm"), lambda p: {"tm": p}


def along_plane():
    def spot():
        sky = lax.axis_index("sky")
        return lax.div(sky, 8) * 2 + lax.rem(sky, 2)

    def name(p):
        depth = lax.rem(lax.div(lax.axis_index("sky"), 2), 4)
        return {"sky": lax.div(p, 2) * 8 + depth * 2 + lax.rem(p, 2)}

    return 8, spot, name


def along_depth():
    def spot():
        return lax.rem(lax.div(lax.axis_index("sky"), 2), 4)

    def name(p):
        sky = lax.axis_index("sky")
        return {"sky": lax.div(sky, 8) * 8 + p * 2 + lax.rem(sky, 2)}

    return 4, spot, name


def signal_all(barrier, group):
    count, spot, name = group
    me = spot()
    for step in range(1, count):
        peer = lax.rem(me + step, count)
        pl.semaphore_signal(barrier, inc=1, device_id=name(peer), device_id_type=MESH)
    return count - 1


def send_all(group, source, land, send_sem, recv_sem):
    count, spot, name = group
    me = spot()
    copies = []
    for step in range(1, count):
        peer = lax.rem(me + step, count)
        copy = pltpu.make_async_remote_copy(
            src_ref=source(peer),
            dst_ref=land.at[step - 1],
            send_sem=send_sem.at[step - 1],
            recv_sem=recv_sem.at[step - 1],
            device_id=name(peer),
            device_id_type=MESH,
        )
        copy.start()
        copies.append(copy)
    return copies


def finish_sends(copies):
    for copy in copies:
        copy.wait_send()


def finish_sum(group, copies, x_ref, land):
    total = x_ref[group[1]()]
    for step, copy in enumerate(copies):
        copy.wait_recv()
        total = total + land[step]
    finish_sends(copies)
    return total


def finish_spread(group, copies, x_ref, land, place):
    count, spot, _ = group
    me = spot()
    place(me, x_ref[...])
    for step, copy in enumerate(copies):
        copy.wait_recv()
        place(lax.rem(me + count - step - 1, count), land[step])
    finish_sends(copies)


def start_sum(group, x_ref, stage):
    return send_all(group, lambda peer: x_ref.at[peer], *stage)


def start_spread(group, x_ref, stage):
    return send_all(group, lambda peer: x_ref, *stage)


def finish_ordered(group, copies, x_ref, land, held):
    def place(position, block):
        held[position] = block

    finish_spread(group, copies, x_ref, land, place)
    total = held[0]
    for position in range(1, group[0]):
        total = total + held[position]
    return total


def neighbours(source, land, send_sem, recv_sem, count):
    me = lax.axis_index("tm")
    after, before = lax.rem(me + 1, count), lax.rem(me + count - 1, count)
    return [
        pltpu.make_async_remote_copy(
            src_ref=source,
            dst_ref=land.at[side],
            send_sem=send_sem.at[side],
            recv_sem=recv_sem.at[side],
            device_id={"tm": peer},
            device_id_type=MESH,
        )
        for side, peer in enumerate((after, before))
    ]


def start_sides(source, stage, count):
    me = lax.axis_index("tm")
    ahead, behind = neighbours(source, *stage, count)
    pl.when(me < count - 1)(ahead.start)
    pl.when(me > 0)(behind.start)
    return ahead, behind


def finish_sides(copies, source, land, count):
    me = lax.axis_index("tm")
    has_before, has_after = me > 0, me < count - 1
    ahead, behind = copies
    pl.when(has_before)(ahead.wait_recv)
    pl.when(has_after)(behind.wait_recv)
    pl.when(has_after)(ahead.wait_send)
    pl.when(has_before)(behind.wait_send)
    own = source[...]
    lanes = lax.broadcasted_iota(jnp.int32, own.shape, 1)
    half = own.shape[1] // 2
    halo = jnp.where(jnp.logical_and(lanes < half, has_after), land[1], own)
    halo = jnp.where(jnp.logical_and(lanes >= half, has_before), land[0], halo)
    return jnp.concatenate([own, halo], axis=1)


def stage_scratch(group, block):
    peers = group[0] - 1
    return [
        pltpu.VMEM((peers,) + block, jnp.float32),
        pltpu.SemaphoreType.DMA((peers,)),
        pltpu.SemaphoreType.DMA((peers,)),
    ]


def side_scratch(block):
    return [
        pltpu.VMEM((2,) + block, jnp.float32),
        pltpu.SemaphoreType.DMA((2,)),
        pltpu.SemaphoreType.DMA((2,)),
    ]


def solve_sources(moments):
    matrix = {}
    for position, pair in enumerate(LOWER_PAIRS):
        matrix[pair] = moments[position] + (1.0 if pair[0] == pair[1] else 0.0)
    factor = {}
    for i in range(5):
        for j in range(i + 1):
            reduced = matrix[i, j]
            for k in range(j):
                reduced = reduced - factor[i, k] * factor[j, k]
            if i == j:
                factor[i, i] = jnp.sqrt(reduced)
            else:
                factor[i, j] = reduced / factor[j, j]
    forward = []
    for i in range(5):
        current = moments[15 + i]
        for k in range(i):
            current = current - factor[i, k] * forward[k]
        forward.append(current / factor[i, i])
    result = [None] * 5
    for i in reversed(range(5)):
        current = forward[i]
        for k in range(i + 1, 5):
            current = current - factor[k, i] * result[k]
        result[i] = current / factor[i, i]
    return result


CHUNK = 1024
LOW = 256
ROWS = 24


def two_parts(values):
    high = values.astype(jnp.bfloat16)
    return high, (values - high.astype(jnp.float32)).astype(jnp.bfloat16)


def chosen(index, count):
    ids = lax.broadcasted_iota(jnp.int32, (count, index.shape[1]), 0)
    return (ids == index).astype(jnp.float32)


def applied(inverse, vector, knots):
    parts = [None] * 4
    for row in range(knots):
        term = inverse[row] * vector[row : row + 1, :]
        spot = row % 4
        parts[spot] = term if parts[spot] is None else parts[spot] + term
    return (parts[0] + parts[1]) + (parts[2] + parts[3])


def update_kernel(
    knots,
    group,
    residuals_ref,
    weights_ref,
    partials_ref,
    index_ref,
    sources_ref,
    blocks_ref,
    ties_ref,
    attitude_ref,
    window_ref,
    new_ref,
    o_ref,
    total_ref,
    moments,
    solved_ref,
    changes,
    quarters,
    corner,
    eighth,
    packed_ref,
    rhs_ref,
    rhs_part,
    rhs_plane,
    rhs_depth,
    inverse,
    wide_corner,
    rhs_total,
    *scratch,
):
    stages = [scratch[i : i + 3] for i in range(0, len(scratch), 3)]
    plane, depth = along_plane(), along_depth()
    count = group[0]
    barrier = pltpu.get_barrier_semaphore()
    peers = signal_all(barrier, group) + signal_all(barrier, plane) + signal_all(barrier, depth)
    chunks = residuals_ref.shape[1] // CHUNK
    total_ref[...] = jnp.zeros_like(total_ref)

    def gather_sums(chunk, carry):
        span = pl.ds(pl.multiple_of(chunk * CHUNK, CHUNK), CHUNK)
        index = index_ref[:, span]
        weights = weights_ref[:, span]
        residuals = residuals_ref[:, span]
        values = partials_ref[:, span].astype(jnp.float32)
        rows = [values[i : i + 1, :] for i in range(5)]
        scaled = [weights * row for row in rows]
        entries = [scaled[i] * rows[j] for i, j in LOWER_PAIRS]
        entries = entries + [scaled[i] * residuals for i in range(5)]
        entries = entries + [jnp.zeros_like(weights)] * (ROWS - 20)
        high, low = two_parts(jnp.concatenate(entries, axis=0))
        both = jnp.concatenate([high, low], axis=0)
        owner = chosen(lax.div(index, LOW), count)
        held = [both * owner[h : h + 1, :].astype(jnp.bfloat16) for h in range(count)]
        held = jnp.concatenate(held, axis=0)
        picks = chosen(lax.rem(index, LOW), LOW).astype(jnp.bfloat16)
        total_ref[...] += lax.dot_general(
            held, picks, (((1,), (1,)), ((), ())), preferred_element_type=jnp.float32
        )
        return carry

    lax.fori_loop(0, chunks, gather_sums, 0)
    for h in range(count):
        start = 2 * ROWS * h
        moments[h] = total_ref[start : start + ROWS] + total_ref[start + ROWS : start + 2 * ROWS]

    pl.semaphore_wait(barrier, peers)
    plane_sum = start_sum(plane, blocks_ref, stages[2])
    time_sum = start_sum(group, moments, stages[0])

    total = finish_sum(plane, plane_sum, blocks_ref, stages[2][0])
    for part in range(depth[0]):
        quarters[part] = total[PIECE * part : PIECE * (part + 1)]
    depth_sum = start_sum(depth, quarters, stages[3])

    total = finish_sum(group, time_sum, moments, stages[0][0])
    solved = solve_sources([total[r : r + 1, :] for r in range(20)])
    zero = jnp.zeros_like(solved[0])
    solved_ref[...] = jnp.concatenate(solved + [zero] * 3, axis=0)
    time_spread = start_spread(group, solved_ref, stages[1])

    corner[:PIECE, :] = finish_sum(depth, depth_sum, quarters, stages[3][0])
    corner[PIECE:, :] = jnp.concatenate([ties_ref[...]] + [jnp.zeros_like(ties_ref[...])] * 3, axis=0)
    corner_sides = start_sides(corner, stages[8], count)

    def place(position, block):
        span = pl.ds(pl.multiple_of(position * LOW, LOW), LOW)
        new_ref[:, span] = sources_ref[:, span] + block[:5]
        changes[position] = block

    finish_spread(group, time_spread, solved_ref, stages[1][0], place)
    wide = finish_sides(corner_sides, corner, stages[8][0], count)
    wide_corner[...] = wide[:PIECE]
    depth_spread = start_spread(depth, wide_corner, stages[4])
    left, right = wide[PIECE : PIECE + 1], wide[PIECE + 1 : PIECE + 2]
    table = changes[...].reshape(count * 8, LOW)
    high, low = two_parts(table)

    def use_changes(chunk, carry):
        span = pl.ds(pl.multiple_of(chunk * CHUNK, CHUNK), CHUNK)
        index = index_ref[:, span]
        owner = chosen(lax.div(index, LOW), count)
        picks = chosen(lax.rem(index, LOW), LOW).astype(jnp.bfloat16)
        found = jnp.dot(high, picks, preferred_element_type=jnp.float32)
        found = found + jnp.dot(low, picks, preferred_element_type=jnp.float32)
        picked = found[0:8] * owner[0:1]
        for h in range(1, count):
            picked = picked + found[8 * h : 8 * h + 8] * owner[h : h + 1]
        values = partials_ref[:, span].astype(jnp.float32)
        fitted = jnp.sum(values * picked[:5], axis=0, keepdims=True)
        weighted = weights_ref[:, span] * (residuals_ref[:, span] - fitted)
        tied = chosen(window_ref[:, span], lanes) * weighted.astype(jnp.bfloat16).astype(jnp.float32)
        rhs_ref[...] += lax.dot_general(
            attitude_ref[:, span],
            tied.astype(jnp.bfloat16),
            (((1,), (1,)), ((), ())),
            preferred_element_type=jnp.float32,
        )
        return carry

    lanes = ties_ref.shape[1]
    rhs_ref[...] = jnp.zeros_like(rhs_ref)
    lax.fori_loop(0, chunks, use_changes, 0)
    rhs_first = start_spread(plane, rhs_ref, stages[6])

    def place_quarter(position, block):
        eighth[pl.ds(pl.multiple_of(position * PIECE, PIECE), PIECE), :] = block

    finish_spread(depth, depth_spread, wide_corner, stages[4][0], place_quarter)
    plane_spread = start_spread(plane, eighth, stages[5])
    rhs_part[...] = finish_ordered(plane, rhs_first, rhs_ref, stages[6][0], rhs_plane)
    rhs_second = start_spread(depth, rhs_part, stages[7])
    width = depth[0] * PIECE

    def place_eighth(position, block):
        packed_ref[pl.ds(pl.multiple_of(position * width, width), width), :] = block

    rhs_total[...] = finish_ordered(depth, rhs_second, rhs_part, stages[7][0], rhs_depth)
    rhs_sides = start_sides(rhs_total, stages[9], count)
    finish_spread(plane, plane_spread, eighth, stages[5][0], place_eighth)

    row_ids = lax.broadcasted_iota(jnp.int32, (knots, 2 * lanes), 0)
    start = 0
    for group in range(knots // BLOCK):
        width = (group + 1) * BLOCK
        for k in range(group * BLOCK, width):
            row = packed_ref[start : start + width, :]
            row = row + jnp.where(row_ids[:width] == k, left + right, 0.0)
            inverse[k, :width, :] = row
            start += width
    for low in range(knots // BLOCK):
        for high in range(low + 1, knots // BLOCK):
            rows = pl.ds(high * BLOCK, BLOCK)
            for k in range(low * BLOCK, (low + 1) * BLOCK):
                inverse[k, rows, :] = inverse[rows, k, :]

    def pivot(p, carry):
        own = inverse[p]
        here = row_ids == p
        scale = 1.0 / inverse[p, pl.ds(p, 1), :]
        row = jnp.where(here, scale, own * scale)
        factors = jnp.where(row_ids < p, -own, own)
        for i in range(knots):
            inverse[i] = jnp.where(here, 0.0, inverse[i]) - factors[i : i + 1, :] * row
        inverse[p] = row
        return carry

    lax.fori_loop(0, knots, pivot, 0)

    right_side = finish_sides(rhs_sides, rhs_total, stages[9][0], count)
    base = DAMPING * applied(inverse, right_side, knots)
    change = base
    for _ in range(ITERS - 1):
        tied = left * pltpu.roll(change, 1, 1) + right * pltpu.roll(change, 2 * lanes - 1, 1)
        change = (1.0 - DAMPING) * change + base + DAMPING * applied(inverse, tied, knots)
    o_ref[...] = change[:, :lanes]


def updates(residuals, weights, partials, index, sources, blocks, ties, attitude, window, group):
    knots, lanes, count = attitude.shape[0], ties.shape[1], group[0]
    plane, depth = along_plane(), along_depth()
    piece, whole, side = (PIECE, lanes), (depth[0] * PIECE, lanes), (knots, lanes)

    def held(*shape):
        return pltpu.VMEM(shape, jnp.float32)

    return pl.pallas_call(
        functools.partial(update_kernel, knots, group),
        name="updates",
        out_shape=(
            jax.ShapeDtypeStruct(sources.shape, jnp.float32),
            jax.ShapeDtypeStruct(side, jnp.float32),
        ),
        in_specs=[VMEM] * 9,
        out_specs=(VMEM, VMEM),
        scratch_shapes=[
            held(count * 2 * ROWS, LOW),
            held(count, ROWS, LOW),
            held(8, LOW),
            held(count, 8, LOW),
            held(depth[0], *piece),
            held(PIECE + 8, lanes),
            held(whole[0], 2 * lanes),
            held(plane[0] * whole[0], 2 * lanes),
            held(*side),
            held(*side),
            held(plane[0], *side),
            held(depth[0], *side),
            held(knots, knots, 2 * lanes),
            held(PIECE, 2 * lanes),
            held(*side),
        ]
        + stage_scratch(group, (ROWS, LOW))
        + stage_scratch(group, (8, LOW))
        + stage_scratch(plane, whole)
        + stage_scratch(depth, piece)
        + stage_scratch(depth, (PIECE, 2 * lanes))
        + stage_scratch(plane, (whole[0], 2 * lanes))
        + stage_scratch(plane, side)
        + stage_scratch(depth, side)
        + side_scratch((PIECE + 8, lanes))
        + side_scratch(side),
        compiler_params=pltpu.CompilerParams(
            collective_id=1, has_side_effects=True, vmem_limit_bytes=48 << 20
        ),
    )(residuals[None], weights[None], partials, index[None], sources, blocks, ties, attitude, window[None])


def on_device(
    residuals,
    weights,
    source_partials,
    attitude_partials,
    source_index,
    tile_window,
    sources,
    attitude,
    coupling,
):
    window_count, knot_count = attitude.shape
    tile_count = attitude_partials.shape[1] // TILE
    times = lax.axis_size("tm")
    time_group = along_time(times)

    scaled = (weights[None, :] * attitude_partials.astype(jnp.float32)).astype(jnp.bfloat16)
    shaped_att = attitude_partials.reshape(knot_count, tile_count, TILE)
    tile_normal = jnp.einsum(
        "ktp,ltp->tkl",
        scaled.reshape(knot_count, tile_count, TILE),
        shaped_att,
        preferred_element_type=jnp.float32,
    )
    tile_normal = 0.5 * (tile_normal + jnp.swapaxes(tile_normal, 1, 2))
    tile_lower = jnp.concatenate(
        [
            tile_normal[:, b : b + BLOCK, : b + BLOCK].reshape(tile_count, -1)
            for b in range(0, knot_count, BLOCK)
        ],
        axis=1,
    )

    first_window = lax.axis_index("tm") * window_count
    window_ids = lax.broadcasted_iota(jnp.int32, (tile_count, window_count), 1)
    selector = (tile_window[:, None] - first_window == window_ids).astype(jnp.float32)
    packed = lax.dot_general(
        tile_lower, selector, (((0,), (0,)), ((), ())), precision=HIGHEST
    )
    packed = jnp.pad(packed, ((0, 768 - packed.shape[0]), (0, 0)))

    earlier = lax.ppermute(coupling[-1:], "tm", [(i, i + 1) for i in range(times - 1)])
    left = jnp.concatenate([earlier, coupling[:-1]])
    is_final = lax.axis_index("tm") == times - 1
    final_slot = lax.broadcasted_iota(jnp.int32, (window_count,), 0) == window_count - 1
    right = jnp.where(jnp.logical_and(is_final, final_slot), 0.0, coupling)
    new_sources, change = updates(
        residuals,
        weights,
        source_partials,
        source_index,
        sources,
        packed.reshape(8, 4 * PIECE, window_count),
        jnp.stack([left, right]),
        attitude_partials,
        jnp.broadcast_to((tile_window - first_window)[:, None], (tile_count, TILE)).reshape(-1),
        time_group,
    )
    return (new_sources, attitude + change.T)


def solution(mesh):
    return jax.shard_map(
        on_device,
        mesh=mesh,
        in_specs=(
            P(("sky", "tm")),
            P(("sky", "tm")),
            P(None, ("sky", "tm")),
            P(None, ("sky", "tm")),
            P(("sky", "tm")),
            P(("sky", "tm")),
            P(None, "sky"),
            P("tm", None),
            P("tm"),
        ),
        out_specs=(P(None, "sky"), P("tm", None)),
        check_vma=False,
    )
```

```python
import functools

import jax
import jax.numpy as jnp
from jax import lax
from jax.experimental import pallas as pl
from jax.experimental.pallas import tpu as pltpu
from jax.sharding import PartitionSpec as P

TILE = 128
ITERS = 8
BLOCK = 8
PIECE = 24
USED = 20
LOWER_PAIRS = tuple(((i, j) for i in range(5) for j in range(i + 1)))
DAMPING = 0.8
HIGHEST = lax.Precision.HIGHEST
MESH = pl.DeviceIdType.MESH
VMEM = pl.BlockSpec(memory_space=pltpu.VMEM)


def along_time(count):
    return count, lambda: lax.axis_index("tm"), lambda p: {"tm": p}


def along_plane():
    def spot():
        sky = lax.axis_index("sky")
        return lax.div(sky, 8) * 2 + lax.rem(sky, 2)

    def name(p):
        depth = lax.rem(lax.div(lax.axis_index("sky"), 2), 4)
        return {"sky": lax.div(p, 2) * 8 + depth * 2 + lax.rem(p, 2)}

    return 8, spot, name


def along_depth():
    def spot():
        return lax.rem(lax.div(lax.axis_index("sky"), 2), 4)

    def name(p):
        sky = lax.axis_index("sky")
        return {"sky": lax.div(sky, 8) * 8 + p * 2 + lax.rem(sky, 2)}

    return 4, spot, name


def signal_all(barrier, group):
    count, spot, name = group
    me = spot()
    for step in range(1, count):
        peer = lax.rem(me + step, count)
        pl.semaphore_signal(barrier, inc=1, device_id=name(peer), device_id_type=MESH)
    return count - 1


def send_all(group, source, land, send_sem, recv_sem):
    count, spot, name = group
    me = spot()
    copies = []
    for step in range(1, count):
        peer = lax.rem(me + step, count)
        copy = pltpu.make_async_remote_copy(
            src_ref=source(peer),
            dst_ref=land.at[step - 1],
            send_sem=send_sem.at[step - 1],
            recv_sem=recv_sem.at[step - 1],
            device_id=name(peer),
            device_id_type=MESH,
        )
        copy.start()
        copies.append(copy)
    return copies


def finish_sends(copies):
    for copy in copies:
        copy.wait_send()


def finish_sum(group, copies, x_ref, land):
    total = x_ref[group[1]()]
    for step, copy in enumerate(copies):
        copy.wait_recv()
        total = total + land[step]
    finish_sends(copies)
    return total


def finish_spread(group, copies, x_ref, land, place):
    count, spot, _ = group
    me = spot()
    place(me, x_ref[...])
    for step, copy in enumerate(copies):
        copy.wait_recv()
        place(lax.rem(me + count - step - 1, count), land[step])
    finish_sends(copies)


def start_sum(group, x_ref, stage):
    return send_all(group, lambda peer: x_ref.at[peer], *stage)


def start_spread(group, x_ref, stage):
    return send_all(group, lambda peer: x_ref, *stage)


def finish_ordered(group, copies, x_ref, land, held):
    def place(position, block):
        held[position] = block

    finish_spread(group, copies, x_ref, land, place)
    total = held[0]
    for position in range(1, group[0]):
        total = total + held[position]
    return total


def neighbours(source, land, send_sem, recv_sem, count):
    me = lax.axis_index("tm")
    after, before = lax.rem(me + 1, count), lax.rem(me + count - 1, count)
    return [
        pltpu.make_async_remote_copy(
            src_ref=source,
            dst_ref=land.at[side],
            send_sem=send_sem.at[side],
            recv_sem=recv_sem.at[side],
            device_id={"tm": peer},
            device_id_type=MESH,
        )
        for side, peer in enumerate((after, before))
    ]


def start_sides(source, stage, count):
    me = lax.axis_index("tm")
    ahead, behind = neighbours(source, *stage, count)
    pl.when(me < count - 1)(ahead.start)
    pl.when(me > 0)(behind.start)
    return ahead, behind


def finish_sides(copies, source, land, count):
    me = lax.axis_index("tm")
    has_before, has_after = me > 0, me < count - 1
    ahead, behind = copies
    pl.when(has_before)(ahead.wait_recv)
    pl.when(has_after)(behind.wait_recv)
    pl.when(has_after)(ahead.wait_send)
    pl.when(has_before)(behind.wait_send)
    own = source[...]
    lanes = lax.broadcasted_iota(jnp.int32, own.shape, 1)
    half = own.shape[1] // 2
    halo = jnp.where(jnp.logical_and(lanes < half, has_after), land[1], own)
    halo = jnp.where(jnp.logical_and(lanes >= half, has_before), land[0], halo)
    return jnp.concatenate([own, halo], axis=1)


def stage_scratch(group, block):
    peers = group[0] - 1
    return [
        pltpu.VMEM((peers,) + block, jnp.float32),
        pltpu.SemaphoreType.DMA((peers,)),
        pltpu.SemaphoreType.DMA((peers,)),
    ]


def side_scratch(block):
    return [
        pltpu.VMEM((2,) + block, jnp.float32),
        pltpu.SemaphoreType.DMA((2,)),
        pltpu.SemaphoreType.DMA((2,)),
    ]


def solve_sources(moments):
    matrix = {}
    for position, pair in enumerate(LOWER_PAIRS):
        matrix[pair] = moments[position] + (1.0 if pair[0] == pair[1] else 0.0)
    factor = {}
    for i in range(5):
        for j in range(i + 1):
            reduced = matrix[i, j]
            for k in range(j):
                reduced = reduced - factor[i, k] * factor[j, k]
            if i == j:
                factor[i, i] = jnp.sqrt(reduced)
            else:
                factor[i, j] = reduced / factor[j, j]
    forward = []
    for i in range(5):
        current = moments[15 + i]
        for k in range(i):
            current = current - factor[i, k] * forward[k]
        forward.append(current / factor[i, i])
    result = [None] * 5
    for i in reversed(range(5)):
        current = forward[i]
        for k in range(i + 1, 5):
            current = current - factor[k, i] * result[k]
        result[i] = current / factor[i, i]
    return result


CHUNK = 1024
LOW = 256
ROWS = 24


def two_parts(values):
    high = values.astype(jnp.bfloat16)
    return high, (values - high.astype(jnp.float32)).astype(jnp.bfloat16)


def chosen(index, count):
    ids = lax.broadcasted_iota(jnp.int32, (count, index.shape[1]), 0)
    return (ids == index).astype(jnp.float32)


def applied(inverse, vector, knots):
    parts = [None] * 4
    for row in range(knots):
        term = inverse[row] * vector[row : row + 1, :]
        spot = row % 4
        parts[spot] = term if parts[spot] is None else parts[spot] + term
    return (parts[0] + parts[1]) + (parts[2] + parts[3])


def update_kernel(
    knots,
    group,
    residuals_ref,
    weights_ref,
    partials_ref,
    index_ref,
    sources_ref,
    blocks_ref,
    ties_ref,
    attitude_ref,
    window_ref,
    new_ref,
    o_ref,
    total_ref,
    moments,
    solved_ref,
    changes,
    quarters,
    corner,
    eighth,
    packed_ref,
    rhs_ref,
    rhs_part,
    rhs_plane,
    rhs_depth,
    inverse,
    wide_corner,
    wide_quarters,
    rhs_total,
    *scratch,
):
    stages = [scratch[i : i + 3] for i in range(0, len(scratch), 3)]
    plane, depth = along_plane(), along_depth()
    count = group[0]
    barrier = pltpu.get_barrier_semaphore()
    peers = signal_all(barrier, group) + signal_all(barrier, plane) + signal_all(barrier, depth)
    chunks = residuals_ref.shape[1] // CHUNK
    total_ref[...] = jnp.zeros_like(total_ref)

    def gather_sums(chunk, carry):
        span = pl.ds(pl.multiple_of(chunk * CHUNK, CHUNK), CHUNK)
        index = index_ref[:, span]
        weights = weights_ref[:, span]
        residuals = residuals_ref[:, span]
        values = partials_ref[:, span].astype(jnp.float32)
        rows = [values[i : i + 1, :] for i in range(5)]
        scaled = [weights * row for row in rows]
        entries = [scaled[i] * rows[j] for i, j in LOWER_PAIRS]
        entries = entries + [scaled[i] * residuals for i in range(5)]
        entries = entries + [jnp.zeros_like(weights)] * (ROWS - 20)
        high, low = two_parts(jnp.concatenate(entries, axis=0))
        both = jnp.concatenate([high, low], axis=0)
        owner = chosen(lax.div(index, LOW), count)
        held = [both * owner[h : h + 1, :].astype(jnp.bfloat16) for h in range(count)]
        held = jnp.concatenate(held, axis=0)
        picks = chosen(lax.rem(index, LOW), LOW).astype(jnp.bfloat16)
        total_ref[...] += lax.dot_general(
            held, picks, (((1,), (1,)), ((), ())), preferred_element_type=jnp.float32
        )
        return carry

    early = chunks * 5 // 8
    lax.fori_loop(0, early, gather_sums, 0)
    pl.semaphore_wait(barrier, peers)
    plane_sum = start_sum(plane, blocks_ref, stages[2])
    lax.fori_loop(early, chunks, gather_sums, 0)
    for h in range(count):
        start = 2 * ROWS * h
        moments[h] = total_ref[start : start + ROWS] + total_ref[start + ROWS : start + 2 * ROWS]

    time_sum = start_sum(group, moments, stages[0])

    total = finish_sum(plane, plane_sum, blocks_ref, stages[2][0])
    for part in range(depth[0]):
        quarters[part, :USED, :] = total[USED * part : USED * (part + 1)]
        quarters[part, USED:, :] = jnp.zeros((PIECE - USED, total.shape[1]), jnp.float32)
    depth_sum = start_sum(depth, quarters, stages[3])

    total = finish_sum(group, time_sum, moments, stages[0][0])
    solved = solve_sources([total[r : r + 1, :] for r in range(20)])
    zero = jnp.zeros_like(solved[0])
    solved_ref[...] = jnp.concatenate(solved + [zero] * 3, axis=0)
    time_spread = start_spread(group, solved_ref, stages[1])

    corner[:PIECE, :] = finish_sum(depth, depth_sum, quarters, stages[3][0])
    corner[PIECE:, :] = jnp.broadcast_to(ties_ref[...], (8, ties_ref.shape[1]))
    corner_sides = start_sides(corner, stages[8], count)

    def place(position, block):
        span = pl.ds(pl.multiple_of(position * LOW, LOW), LOW)
        new_ref[:, span] = sources_ref[:, span] + block[:5]
        changes[position] = block

    finish_spread(group, time_spread, solved_ref, stages[1][0], place)
    wide = finish_sides(corner_sides, corner, stages[8][0], count)
    wide_corner[...] = wide[:PIECE]
    depth_spread = start_spread(depth, wide_corner, stages[4])
    right = wide[PIECE : PIECE + 1]
    starts = lax.broadcasted_iota(jnp.int32, right.shape, 1) == 0
    starts = jnp.logical_and(starts, lax.axis_index("tm") == 0)
    left = jnp.where(starts, 0.0, pltpu.roll(jnp.broadcast_to(right, (8, right.shape[1])), 1, 1)[0:1])
    table = changes[...].reshape(count * 8, LOW)
    high, low = two_parts(table)

    def use_changes(chunk, carry):
        span = pl.ds(pl.multiple_of(chunk * CHUNK, CHUNK), CHUNK)
        index = index_ref[:, span]
        owner = chosen(lax.div(index, LOW), count)
        picks = chosen(lax.rem(index, LOW), LOW).astype(jnp.bfloat16)
        found = jnp.dot(high, picks, preferred_element_type=jnp.float32)
        found = found + jnp.dot(low, picks, preferred_element_type=jnp.float32)
        picked = found[0:8] * owner[0:1]
        for h in range(1, count):
            picked = picked + found[8 * h : 8 * h + 8] * owner[h : h + 1]
        values = partials_ref[:, span].astype(jnp.float32)
        fitted = jnp.sum(values * picked[:5], axis=0, keepdims=True)
        weighted = weights_ref[:, span] * (residuals_ref[:, span] - fitted)
        tied = chosen(window_ref[:, span], lanes) * weighted.astype(jnp.bfloat16).astype(jnp.float32)
        rhs_ref[...] += lax.dot_general(
            attitude_ref[:, span],
            tied.astype(jnp.bfloat16),
            (((1,), (1,)), ((), ())),
            preferred_element_type=jnp.float32,
        )
        return carry

    lanes = ties_ref.shape[1]
    rhs_ref[...] = jnp.zeros_like(rhs_ref)
    lax.fori_loop(0, chunks, use_changes, 0)
    rhs_first = start_spread(plane, rhs_ref, stages[6])

    def place_quarter(position, block):
        wide_quarters[position] = block

    finish_spread(depth, depth_spread, wide_corner, stages[4][0], place_quarter)
    for part in range(depth[0]):
        eighth[USED * part : USED * (part + 1), :] = wide_quarters[part, :USED, :]
    plane_spread = start_spread(plane, eighth, stages[5])
    rhs_part[...] = finish_ordered(plane, rhs_first, rhs_ref, stages[6][0], rhs_plane)
    rhs_second = start_spread(depth, rhs_part, stages[7])
    width = depth[0] * USED

    def place_eighth(position, block):
        packed_ref[pl.ds(pl.multiple_of(position * width, width), width), :] = block

    rhs_total[...] = finish_ordered(depth, rhs_second, rhs_part, stages[7][0], rhs_depth)
    rhs_sides = start_sides(rhs_total, stages[9], count)
    finish_spread(plane, plane_spread, eighth, stages[5][0], place_eighth)

    row_ids = lax.broadcasted_iota(jnp.int32, (knots, 2 * lanes), 0)
    start = 0
    for group in range(knots // BLOCK):
        width = (group + 1) * BLOCK
        for k in range(group * BLOCK, width):
            row = packed_ref[start : start + width, :]
            row = row + jnp.where(row_ids[:width] == k, left + right, 0.0)
            inverse[k, :width, :] = row
            start += width
    for low in range(knots // BLOCK):
        for high in range(low + 1, knots // BLOCK):
            rows = pl.ds(high * BLOCK, BLOCK)
            for k in range(low * BLOCK, (low + 1) * BLOCK):
                inverse[k, rows, :] = inverse[rows, k, :]

    def pivot(p, carry):
        own = inverse[p]
        here = row_ids == p
        scale = 1.0 / inverse[p, pl.ds(p, 1), :]
        row = jnp.where(here, scale, own * scale)
        factors = jnp.where(row_ids < p, -own, own)
        for i in range(knots):
            inverse[i] = jnp.where(here, 0.0, inverse[i]) - factors[i : i + 1, :] * row
        inverse[p] = row
        return carry

    lax.fori_loop(0, knots, pivot, 0)

    right_side = finish_sides(rhs_sides, rhs_total, stages[9][0], count)
    base = DAMPING * applied(inverse, right_side, knots)
    change = base
    for _ in range(ITERS - 1):
        tied = left * pltpu.roll(change, 1, 1) + right * pltpu.roll(change, 2 * lanes - 1, 1)
        change = (1.0 - DAMPING) * change + base + DAMPING * applied(inverse, tied, knots)
    o_ref[...] = change[:, :lanes]


def updates(residuals, weights, partials, index, sources, blocks, ties, attitude, window, group):
    knots, lanes, count = attitude.shape[0], ties.shape[1], group[0]
    plane, depth = along_plane(), along_depth()
    piece, whole, side = (PIECE, lanes), (depth[0] * USED, lanes), (knots, lanes)

    def held(*shape):
        return pltpu.VMEM(shape, jnp.float32)

    return pl.pallas_call(
        functools.partial(update_kernel, knots, group),
        name="updates",
        out_shape=(
            jax.ShapeDtypeStruct(sources.shape, jnp.float32),
            jax.ShapeDtypeStruct(side, jnp.float32),
        ),
        in_specs=[VMEM] * 9,
        out_specs=(VMEM, VMEM),
        scratch_shapes=[
            held(count * 2 * ROWS, LOW),
            held(count, ROWS, LOW),
            held(8, LOW),
            held(count, 8, LOW),
            held(depth[0], *piece),
            held(PIECE + 8, lanes),
            held(whole[0], 2 * lanes),
            held(plane[0] * whole[0], 2 * lanes),
            held(*side),
            held(*side),
            held(plane[0], *side),
            held(depth[0], *side),
            held(knots, knots, 2 * lanes),
            held(PIECE, 2 * lanes),
            held(depth[0], PIECE, 2 * lanes),
            held(*side),
        ]
        + stage_scratch(group, (ROWS, LOW))
        + stage_scratch(group, (8, LOW))
        + stage_scratch(plane, whole)
        + stage_scratch(depth, piece)
        + stage_scratch(depth, (PIECE, 2 * lanes))
        + stage_scratch(plane, (whole[0], 2 * lanes))
        + stage_scratch(plane, side)
        + stage_scratch(depth, side)
        + side_scratch((PIECE + 8, lanes))
        + side_scratch(side),
        compiler_params=pltpu.CompilerParams(
            collective_id=1, has_side_effects=True, vmem_limit_bytes=48 << 20
        ),
    )(residuals[None], weights[None], partials, index[None], sources, blocks, ties, attitude, window[None])


def on_device(
    residuals,
    weights,
    source_partials,
    attitude_partials,
    source_index,
    tile_window,
    sources,
    attitude,
    coupling,
):
    window_count, knot_count = attitude.shape
    tile_count = attitude_partials.shape[1] // TILE
    times = lax.axis_size("tm")
    time_group = along_time(times)

    scaled = (weights[None, :] * attitude_partials.astype(jnp.float32)).astype(jnp.bfloat16)
    shaped_att = attitude_partials.reshape(knot_count, tile_count, TILE)
    tile_normal = jnp.einsum(
        "ktp,ltp->tkl",
        scaled.reshape(knot_count, tile_count, TILE),
        shaped_att,
        preferred_element_type=jnp.float32,
    )
    tile_normal = 0.5 * (tile_normal + jnp.swapaxes(tile_normal, 1, 2))
    tile_lower = jnp.concatenate(
        [
            tile_normal[:, b : b + BLOCK, : b + BLOCK].reshape(tile_count, -1)
            for b in range(0, knot_count, BLOCK)
        ],
        axis=1,
    )

    first_window = lax.axis_index("tm") * window_count
    window_ids = lax.broadcasted_iota(jnp.int32, (tile_count, window_count), 1)
    selector = (tile_window[:, None] - first_window == window_ids).astype(jnp.float32)
    packed = lax.dot_general(
        tile_lower, selector, (((0,), (0,)), ((), ())), precision=HIGHEST
    )

    is_final = lax.axis_index("tm") == times - 1
    final_slot = lax.broadcasted_iota(jnp.int32, (window_count,), 0) == window_count - 1
    right = jnp.where(jnp.logical_and(is_final, final_slot), 0.0, coupling)
    new_sources, change = updates(
        residuals,
        weights,
        source_partials,
        source_index,
        sources,
        packed.reshape(8, 4 * USED, window_count),
        right[None],
        attitude_partials,
        jnp.broadcast_to((tile_window - first_window)[:, None], (tile_count, TILE)).reshape(-1),
        time_group,
    )
    return (new_sources, attitude + change.T)


def solution(mesh):
    return jax.shard_map(
        on_device,
        mesh=mesh,
        in_specs=(
            P(("sky", "tm")),
            P(("sky", "tm")),
            P(None, ("sky", "tm")),
            P(None, ("sky", "tm")),
            P(("sky", "tm")),
            P(("sky", "tm")),
            P(None, "sky"),
            P("tm", None),
            P("tm"),
        ),
        out_specs=(P(None, "sky"), P("tm", None)),
        check_vma=False,
    )
```

```python
import functools

import jax
import jax.numpy as jnp
from jax import lax
from jax.experimental import pallas as pl
from jax.experimental.pallas import tpu as pltpu
from jax.sharding import PartitionSpec as P

TILE = 128
ITERS = 8
BLOCK = 8
PIECE = 24
USED = 20
LOWER_PAIRS = tuple(((i, j) for i in range(5) for j in range(i + 1)))
DAMPING = 0.8
HIGHEST = lax.Precision.HIGHEST
MESH = pl.DeviceIdType.MESH
VMEM = pl.BlockSpec(memory_space=pltpu.VMEM)


def along_time(count):
    return count, lambda: lax.axis_index("tm"), lambda p: {"tm": p}


def along_plane():
    def spot():
        sky = lax.axis_index("sky")
        return lax.div(sky, 8) * 2 + lax.rem(sky, 2)

    def name(p):
        depth = lax.rem(lax.div(lax.axis_index("sky"), 2), 4)
        return {"sky": lax.div(p, 2) * 8 + depth * 2 + lax.rem(p, 2)}

    return 8, spot, name


def along_depth():
    def spot():
        return lax.rem(lax.div(lax.axis_index("sky"), 2), 4)

    def name(p):
        sky = lax.axis_index("sky")
        return {"sky": lax.div(sky, 8) * 8 + p * 2 + lax.rem(sky, 2)}

    return 4, spot, name


def signal_all(barrier, group):
    count, spot, name = group
    me = spot()
    for step in range(1, count):
        peer = lax.rem(me + step, count)
        pl.semaphore_signal(barrier, inc=1, device_id=name(peer), device_id_type=MESH)
    return count - 1


def send_all(group, source, land, send_sem, recv_sem):
    count, spot, name = group
    me = spot()
    copies = []
    for step in range(1, count):
        peer = lax.rem(me + step, count)
        copy = pltpu.make_async_remote_copy(
            src_ref=source(peer),
            dst_ref=land.at[step - 1],
            send_sem=send_sem.at[step - 1],
            recv_sem=recv_sem.at[step - 1],
            device_id=name(peer),
            device_id_type=MESH,
        )
        copy.start()
        copies.append(copy)
    return copies


def finish_sends(copies):
    for copy in copies:
        copy.wait_send()


def finish_sum(group, copies, x_ref, land):
    total = x_ref[group[1]()]
    for step, copy in enumerate(copies):
        copy.wait_recv()
        total = total + land[step]
    finish_sends(copies)
    return total


def finish_spread(group, copies, x_ref, land, place):
    count, spot, _ = group
    me = spot()
    place(me, x_ref[...])
    for step, copy in enumerate(copies):
        copy.wait_recv()
        place(lax.rem(me + count - step - 1, count), land[step])
    finish_sends(copies)


def start_sum(group, x_ref, stage):
    return send_all(group, lambda peer: x_ref.at[peer], *stage)


def start_spread(group, x_ref, stage):
    return send_all(group, lambda peer: x_ref, *stage)


def finish_ordered(group, copies, x_ref, land, held):
    def place(position, block):
        held[position] = block

    finish_spread(group, copies, x_ref, land, place)
    total = held[0]
    for position in range(1, group[0]):
        total = total + held[position]
    return total


def neighbours(source, land, send_sem, recv_sem, count):
    me = lax.axis_index("tm")
    after, before = lax.rem(me + 1, count), lax.rem(me + count - 1, count)
    return [
        pltpu.make_async_remote_copy(
            src_ref=source,
            dst_ref=land.at[side],
            send_sem=send_sem.at[side],
            recv_sem=recv_sem.at[side],
            device_id={"tm": peer},
            device_id_type=MESH,
        )
        for side, peer in enumerate((after, before))
    ]


def start_sides(source, stage, count):
    me = lax.axis_index("tm")
    ahead, behind = neighbours(source, *stage, count)
    pl.when(me < count - 1)(ahead.start)
    pl.when(me > 0)(behind.start)
    return ahead, behind


def finish_sides(copies, source, land, count):
    me = lax.axis_index("tm")
    has_before, has_after = me > 0, me < count - 1
    ahead, behind = copies
    pl.when(has_before)(ahead.wait_recv)
    pl.when(has_after)(behind.wait_recv)
    pl.when(has_after)(ahead.wait_send)
    pl.when(has_before)(behind.wait_send)
    own = source[...]
    lanes = lax.broadcasted_iota(jnp.int32, own.shape, 1)
    half = own.shape[1] // 2
    halo = jnp.where(jnp.logical_and(lanes < half, has_after), land[1], own)
    halo = jnp.where(jnp.logical_and(lanes >= half, has_before), land[0], halo)
    return jnp.concatenate([own, halo], axis=1)


def stage_scratch(group, block):
    peers = group[0] - 1
    return [
        pltpu.VMEM((peers,) + block, jnp.float32),
        pltpu.SemaphoreType.DMA((peers,)),
        pltpu.SemaphoreType.DMA((peers,)),
    ]


def side_scratch(block):
    return [
        pltpu.VMEM((2,) + block, jnp.float32),
        pltpu.SemaphoreType.DMA((2,)),
        pltpu.SemaphoreType.DMA((2,)),
    ]


def solve_sources(moments):
    matrix = {}
    for position, pair in enumerate(LOWER_PAIRS):
        matrix[pair] = moments[position] + (1.0 if pair[0] == pair[1] else 0.0)
    factor = {}
    for i in range(5):
        for j in range(i + 1):
            reduced = matrix[i, j]
            for k in range(j):
                reduced = reduced - factor[i, k] * factor[j, k]
            if i == j:
                factor[i, i] = jnp.sqrt(reduced)
            else:
                factor[i, j] = reduced / factor[j, j]
    forward = []
    for i in range(5):
        current = moments[15 + i]
        for k in range(i):
            current = current - factor[i, k] * forward[k]
        forward.append(current / factor[i, i])
    result = [None] * 5
    for i in reversed(range(5)):
        current = forward[i]
        for k in range(i + 1, 5):
            current = current - factor[k, i] * result[k]
        result[i] = current / factor[i, i]
    return result


CHUNK = 1024
LOW = 256
ROWS = 24


def two_parts(values):
    high = values.astype(jnp.bfloat16)
    return high, (values - high.astype(jnp.float32)).astype(jnp.bfloat16)


def chosen(index, count):
    ids = lax.broadcasted_iota(jnp.int32, (count, index.shape[1]), 0)
    return (ids == index).astype(jnp.float32)


def applied(inverse, vector, knots):
    parts = [None] * 4
    for row in range(knots):
        term = inverse[row] * vector[row : row + 1, :]
        spot = row % 4
        parts[spot] = term if parts[spot] is None else parts[spot] + term
    return (parts[0] + parts[1]) + (parts[2] + parts[3])


def update_kernel(
    knots,
    group,
    residuals_ref,
    weights_ref,
    partials_ref,
    index_ref,
    sources_ref,
    blocks_ref,
    ties_ref,
    attitude_ref,
    window_ref,
    new_ref,
    o_ref,
    total_ref,
    moments,
    solved_ref,
    changes,
    quarters,
    corner,
    eighth,
    packed_ref,
    rhs_ref,
    rhs_part,
    rhs_plane,
    rhs_depth,
    inverse,
    wide_corner,
    wide_quarters,
    rhs_total,
    *scratch,
):
    stages = [scratch[i : i + 3] for i in range(0, len(scratch), 3)]
    plane, depth = along_plane(), along_depth()
    count = group[0]
    barrier = pltpu.get_barrier_semaphore()
    peers = signal_all(barrier, group) + signal_all(barrier, plane) + signal_all(barrier, depth)
    chunks = residuals_ref.shape[1] // CHUNK
    total_ref[...] = jnp.zeros_like(total_ref)

    def gather_sums(chunk, carry):
        span = pl.ds(pl.multiple_of(chunk * CHUNK, CHUNK), CHUNK)
        index = index_ref[:, span]
        weights = weights_ref[:, span]
        residuals = residuals_ref[:, span]
        values = partials_ref[:, span].astype(jnp.float32)
        rows = [values[i : i + 1, :] for i in range(5)]
        scaled = [weights * row for row in rows]
        entries = [scaled[i] * rows[j] for i, j in LOWER_PAIRS]
        entries = entries + [scaled[i] * residuals for i in range(5)]
        entries = entries + [jnp.zeros_like(weights)] * (ROWS - 20)
        high, low = two_parts(jnp.concatenate(entries, axis=0))
        both = jnp.concatenate([high, low], axis=0)
        owner = chosen(lax.div(index, LOW), count)
        held = [both * owner[h : h + 1, :].astype(jnp.bfloat16) for h in range(count)]
        held = jnp.concatenate(held, axis=0)
        picks = chosen(lax.rem(index, LOW), LOW).astype(jnp.bfloat16)
        total_ref[...] += lax.dot_general(
            held, picks, (((1,), (1,)), ((), ())), preferred_element_type=jnp.float32
        )
        return carry

    early = chunks * 5 // 8
    lax.fori_loop(0, early, gather_sums, 0)
    pl.semaphore_wait(barrier, peers)
    plane_sum = start_sum(plane, blocks_ref, stages[2])
    lax.fori_loop(early, chunks, gather_sums, 0)
    for h in range(count):
        start = 2 * ROWS * h
        moments[h] = total_ref[start : start + ROWS] + total_ref[start + ROWS : start + 2 * ROWS]

    time_sum = start_sum(group, moments, stages[0])

    total = finish_sum(plane, plane_sum, blocks_ref, stages[2][0])
    for part in range(depth[0]):
        quarters[part, :USED, :] = total[USED * part : USED * (part + 1)]
        quarters[part, USED:, :] = jnp.zeros((PIECE - USED, total.shape[1]), jnp.float32)
    depth_sum = start_sum(depth, quarters, stages[3])

    total = finish_sum(group, time_sum, moments, stages[0][0])
    solved = solve_sources([total[r : r + 1, :] for r in range(20)])
    zero = jnp.zeros_like(solved[0])
    solved_ref[...] = jnp.concatenate(solved + [zero] * 3, axis=0)
    time_spread = start_spread(group, solved_ref, stages[1])

    corner[:PIECE, :] = finish_sum(depth, depth_sum, quarters, stages[3][0])
    corner[PIECE:, :] = jnp.broadcast_to(ties_ref[...], (8, ties_ref.shape[1]))
    corner_sides = start_sides(corner, stages[8], count)

    def place(position, block):
        span = pl.ds(pl.multiple_of(position * LOW, LOW), LOW)
        new_ref[:, span] = sources_ref[:, span] + block[:5]
        changes[position] = block

    wide = finish_sides(corner_sides, corner, stages[8][0], count)
    wide_corner[...] = wide[:PIECE]
    depth_spread = start_spread(depth, wide_corner, stages[4])
    right = wide[PIECE : PIECE + 1]
    starts = lax.broadcasted_iota(jnp.int32, right.shape, 1) == 0
    starts = jnp.logical_and(starts, lax.axis_index("tm") == 0)
    left = jnp.where(starts, 0.0, pltpu.roll(jnp.broadcast_to(right, (8, right.shape[1])), 1, 1)[0:1])
    finish_spread(group, time_spread, solved_ref, stages[1][0], place)
    table = changes[...].reshape(count * 8, LOW)
    high, low = two_parts(table)

    def use_changes(chunk, carry):
        span = pl.ds(pl.multiple_of(chunk * CHUNK, CHUNK), CHUNK)
        index = index_ref[:, span]
        owner = chosen(lax.div(index, LOW), count)
        picks = chosen(lax.rem(index, LOW), LOW).astype(jnp.bfloat16)
        found = jnp.dot(high, picks, preferred_element_type=jnp.float32)
        found = found + jnp.dot(low, picks, preferred_element_type=jnp.float32)
        picked = found[0:8] * owner[0:1]
        for h in range(1, count):
            picked = picked + found[8 * h : 8 * h + 8] * owner[h : h + 1]
        values = partials_ref[:, span].astype(jnp.float32)
        fitted = jnp.sum(values * picked[:5], axis=0, keepdims=True)
        weighted = weights_ref[:, span] * (residuals_ref[:, span] - fitted)
        tied = chosen(window_ref[:, span], lanes) * weighted.astype(jnp.bfloat16).astype(jnp.float32)
        rhs_ref[...] += lax.dot_general(
            attitude_ref[:, span],
            tied.astype(jnp.bfloat16),
            (((1,), (1,)), ((), ())),
            preferred_element_type=jnp.float32,
        )
        return carry

    lanes = ties_ref.shape[1]
    rhs_ref[...] = jnp.zeros_like(rhs_ref)
    lax.fori_loop(0, chunks, use_changes, 0)
    rhs_first = start_spread(plane, rhs_ref, stages[6])

    def place_quarter(position, block):
        wide_quarters[position] = block

    finish_spread(depth, depth_spread, wide_corner, stages[4][0], place_quarter)
    for part in range(depth[0]):
        eighth[USED * part : USED * (part + 1), :] = wide_quarters[part, :USED, :]
    plane_spread = start_spread(plane, eighth, stages[5])
    rhs_part[...] = finish_ordered(plane, rhs_first, rhs_ref, stages[6][0], rhs_plane)
    rhs_second = start_spread(depth, rhs_part, stages[7])
    width = depth[0] * USED

    def place_eighth(position, block):
        packed_ref[pl.ds(pl.multiple_of(position * width, width), width), :] = block

    rhs_total[...] = finish_ordered(depth, rhs_second, rhs_part, stages[7][0], rhs_depth)
    rhs_sides = start_sides(rhs_total, stages[9], count)
    finish_spread(plane, plane_spread, eighth, stages[5][0], place_eighth)

    row_ids = lax.broadcasted_iota(jnp.int32, (knots, 2 * lanes), 0)
    start = 0
    for group in range(knots // BLOCK):
        width = (group + 1) * BLOCK
        for k in range(group * BLOCK, width):
            row = packed_ref[start : start + width, :]
            row = row + jnp.where(row_ids[:width] == k, left + right, 0.0)
            inverse[k, :width, :] = row
            start += width
    for low in range(knots // BLOCK):
        for high in range(low + 1, knots // BLOCK):
            rows = pl.ds(high * BLOCK, BLOCK)
            for k in range(low * BLOCK, (low + 1) * BLOCK):
                inverse[k, rows, :] = inverse[rows, k, :]

    def pivot(p, carry):
        own = inverse[p]
        here = row_ids == p
        scale = 1.0 / inverse[p, pl.ds(p, 1), :]
        row = jnp.where(here, scale, own * scale)
        factors = jnp.where(row_ids < p, -own, own)
        for i in range(knots):
            inverse[i] = jnp.where(here, 0.0, inverse[i]) - factors[i : i + 1, :] * row
        inverse[p] = row
        return carry

    lax.fori_loop(0, knots, pivot, 0)

    right_side = finish_sides(rhs_sides, rhs_total, stages[9][0], count)
    base = DAMPING * applied(inverse, right_side, knots)
    change = base
    for _ in range(ITERS - 1):
        tied = left * pltpu.roll(change, 1, 1) + right * pltpu.roll(change, 2 * lanes - 1, 1)
        change = (1.0 - DAMPING) * change + base + DAMPING * applied(inverse, tied, knots)
    o_ref[...] = change[:, :lanes]


def updates(residuals, weights, partials, index, sources, blocks, ties, attitude, window, group):
    knots, lanes, count = attitude.shape[0], ties.shape[1], group[0]
    plane, depth = along_plane(), along_depth()
    piece, whole, side = (PIECE, lanes), (depth[0] * USED, lanes), (knots, lanes)

    def held(*shape):
        return pltpu.VMEM(shape, jnp.float32)

    return pl.pallas_call(
        functools.partial(update_kernel, knots, group),
        name="updates",
        out_shape=(
            jax.ShapeDtypeStruct(sources.shape, jnp.float32),
            jax.ShapeDtypeStruct(side, jnp.float32),
        ),
        in_specs=[VMEM] * 9,
        out_specs=(VMEM, VMEM),
        scratch_shapes=[
            held(count * 2 * ROWS, LOW),
            held(count, ROWS, LOW),
            held(8, LOW),
            held(count, 8, LOW),
            held(depth[0], *piece),
            held(PIECE + 8, lanes),
            held(whole[0], 2 * lanes),
            held(plane[0] * whole[0], 2 * lanes),
            held(*side),
            held(*side),
            held(plane[0], *side),
            held(depth[0], *side),
            held(knots, knots, 2 * lanes),
            held(PIECE, 2 * lanes),
            held(depth[0], PIECE, 2 * lanes),
            held(*side),
        ]
        + stage_scratch(group, (ROWS, LOW))
        + stage_scratch(group, (8, LOW))
        + stage_scratch(plane, whole)
        + stage_scratch(depth, piece)
        + stage_scratch(depth, (PIECE, 2 * lanes))
        + stage_scratch(plane, (whole[0], 2 * lanes))
        + stage_scratch(plane, side)
        + stage_scratch(depth, side)
        + side_scratch((PIECE + 8, lanes))
        + side_scratch(side),
        compiler_params=pltpu.CompilerParams(
            collective_id=1, has_side_effects=True, vmem_limit_bytes=48 << 20
        ),
    )(residuals[None], weights[None], partials, index[None], sources, blocks, ties, attitude, window[None])


def on_device(
    residuals,
    weights,
    source_partials,
    attitude_partials,
    source_index,
    tile_window,
    sources,
    attitude,
    coupling,
):
    window_count, knot_count = attitude.shape
    tile_count = attitude_partials.shape[1] // TILE
    times = lax.axis_size("tm")
    time_group = along_time(times)

    scaled = (weights[None, :] * attitude_partials.astype(jnp.float32)).astype(jnp.bfloat16)
    shaped_att = attitude_partials.reshape(knot_count, tile_count, TILE)
    tile_normal = jnp.einsum(
        "ktp,ltp->tkl",
        scaled.reshape(knot_count, tile_count, TILE),
        shaped_att,
        preferred_element_type=jnp.float32,
    )
    tile_normal = 0.5 * (tile_normal + jnp.swapaxes(tile_normal, 1, 2))
    tile_lower = jnp.concatenate(
        [
            tile_normal[:, b : b + BLOCK, : b + BLOCK].reshape(tile_count, -1)
            for b in range(0, knot_count, BLOCK)
        ],
        axis=1,
    )

    first_window = lax.axis_index("tm") * window_count
    window_ids = lax.broadcasted_iota(jnp.int32, (tile_count, window_count), 1)
    selector = (tile_window[:, None] - first_window == window_ids).astype(jnp.float32)
    packed = lax.dot_general(
        tile_lower, selector, (((0,), (0,)), ((), ())), precision=HIGHEST
    )

    is_final = lax.axis_index("tm") == times - 1
    final_slot = lax.broadcasted_iota(jnp.int32, (window_count,), 0) == window_count - 1
    right = jnp.where(jnp.logical_and(is_final, final_slot), 0.0, coupling)
    new_sources, change = updates(
        residuals,
        weights,
        source_partials,
        source_index,
        sources,
        packed.reshape(8, 4 * USED, window_count),
        right[None],
        attitude_partials,
        jnp.broadcast_to((tile_window - first_window)[:, None], (tile_count, TILE)).reshape(-1),
        time_group,
    )
    return (new_sources, attitude + change.T)


def solution(mesh):
    return jax.shard_map(
        on_device,
        mesh=mesh,
        in_specs=(
            P(("sky", "tm")),
            P(("sky", "tm")),
            P(None, ("sky", "tm")),
            P(None, ("sky", "tm")),
            P(("sky", "tm")),
            P(("sky", "tm")),
            P(None, "sky"),
            P("tm", None),
            P("tm"),
        ),
        out_specs=(P(None, "sky"), P("tm", None)),
        check_vma=False,
    )
```
